512 devices in a mesh: dop: 32 (over z, x), rng: 16 (over y, core).
Axes of the slice: x: 4, y: 8, z: 8, core: 2. Of those that a mesh axis runs over, the one named last changes fastest.
Arguments:
- raw_samples: bfloat16 [256, 384, 2, 4096], P('dop', 'rng'), may hold values from -16 to 16
- filter_taps: float32 [8, 512], replicated, may hold values from -2 to 2
- range_code: float32 [2, 7], replicated, may hold values from -1.6 to 1.6
- train_mask: int32 [64, 384], P('dop', 'rng'), may hold values 0 or 1
- steer_index: int32 [64, 4], P('dop'), may hold values from 0 to 255
Outputs:
- beam_out: float32 [2, 64, 4, 384], P(None, 'dop', None, 'rng')
The draws below stay inside these ranges and needn't reach their ends.
All inputs are finite; a program needn't handle non-finite values. No bound on the sum of `train_mask` on one device may be relied on, other than what follows from the above.
Results may differ from the reference program's by a relative error of at most 0.012.
The reference program's roundings to bfloat16 on the way (of `filtered`, `dft_table`, `spectra` and `compressed`) count: a program that leaves them out, or rounds other values in their place, can miss the bound.
Values may be sent and summed in bfloat16 or wider, within the bound.
No kernel may reach another device: no remote copies, remote signals or barrier semaphores. Data moves between devices by JAX's collectives and lax.ppermute only.
A program may use at most 64 MiB of HBM per device.

```python
import math
import jax
import jax.numpy as jnp
from jax import lax

ELEMENTS = 256
CHANNELS = 512
TAPS = 8
CODE_REACH = 3
BEAMS = 4
PULSES = 4096
BINS = 64
GATES = 384


def draw_raw_samples(key, part):
    source_count = max(ELEMENTS // 4, 4)
    strongest = 4.0
    decades = 3.5
    direction_key = jax.random.fold_in(key, 11)
    power_key = jax.random.fold_in(key, 12)
    signal_key = jax.random.fold_in(key, 13)
    noise_key = jax.random.fold_in(key, 14)
    sine_values = jax.random.uniform(direction_key, (source_count,), jnp.float32, -0.95, 0.95)
    spacing = (jnp.arange(source_count, dtype=jnp.float32) + jax.random.uniform(power_key, (source_count,), jnp.float32)) / source_count
    amplitude = jnp.sqrt(0.5 * strongest * 10.0 ** (-decades * spacing))
    positions = jnp.arange(ELEMENTS, dtype=jnp.float32)
    phases = math.pi * positions[:, None] * sine_values[None, :]
    cosine = jnp.cos(phases) * amplitude[None, :]
    sine_part = jnp.sin(phases) * amplitude[None, :]
    real_row = jnp.stack([cosine, -sine_part], axis=2)
    imag_row = jnp.stack([sine_part, cosine], axis=2)
    mixing = jnp.stack([real_row, imag_row], axis=1).reshape(2 * ELEMENTS, 2 * source_count)

    def one_gate(gate_number):
        source_key = jax.random.fold_in(signal_key, gate_number)
        floor_key = jax.random.fold_in(noise_key, gate_number)
        sources = jax.random.normal(source_key, (2 * source_count, PULSES), jnp.float32)
        noise_part = jax.random.normal(floor_key, (2 * ELEMENTS, PULSES), jnp.float32) * math.sqrt(0.5)
        combined = jnp.dot(mixing, sources, precision=lax.Precision.HIGHEST) + noise_part
        return jnp.clip(combined, -16.0, 16.0).reshape(ELEMENTS, 2, PULSES).astype(jnp.bfloat16)
    per_gate = lax.map(one_gate, jnp.arange(GATES, dtype=jnp.int32))
    return jnp.transpose(per_gate, (1, 0, 2, 3))


def set_ends(array, key, low, high):
    spot = [jax.random.randint(jax.random.fold_in(key, axis), (), 0, length) for axis, length in enumerate(array.shape)]
    longest = array.shape.index(max(array.shape))
    neighbour = spot[:longest] + [(spot[longest] + 1) % array.shape[longest]] + spot[longest + 1:]
    return array.at[tuple(spot)].set(low).at[tuple(neighbour)].set(high)


def noise(stream_key, dims, width, limit, held_as=jnp.bfloat16):
    return jnp.clip(width * jax.random.normal(stream_key, dims, jnp.float32), -limit, limit).astype(held_as)


def setup_inputs(seed: int = 0) -> dict:
    key_of = jax.random.split(jax.random.key(seed), 6)
    raw_samples = draw_raw_samples(jax.random.fold_in(key_of[5], 71), 0)
    filter_taps = noise(key_of[1], (TAPS, CHANNELS), TAPS ** -0.5, 2.0, jnp.float32)
    range_code = noise(key_of[2], (2, 2 * CODE_REACH + 1), 0.27, 1.6, jnp.float32)
    train_mask = set_ends((jax.random.randint(key_of[3], (BINS, GATES), 0, 4) < 3).astype(jnp.int32), jax.random.fold_in(key_of[3], 1), 0, 1)
    steer_index = set_ends(jax.random.randint(key_of[4], (BINS, BEAMS), 0, ELEMENTS), jax.random.fold_in(key_of[4], 1), 0, ELEMENTS - 1).astype(jnp.int32)
    return {"raw_samples": raw_samples, "filter_taps": filter_taps, "range_code": range_code, "train_mask": train_mask, "steer_index": steer_index}


loading_level = 0.25

def dft_table(bin_total):
    mode_index = jnp.arange(CHANNELS, dtype=jnp.int32)
    bin_index = jnp.arange(bin_total, dtype=jnp.int32)
    turn_count = jnp.mod(mode_index[:, None] * bin_index[None, :], CHANNELS).astype(jnp.float32)
    phases = turn_count * (2.0 * math.pi / CHANNELS)
    cosine = jnp.cos(phases) / math.sqrt(CHANNELS)
    sine_part = jnp.sin(phases) / math.sqrt(CHANNELS)
    top_half = jnp.concatenate([cosine, -sine_part], axis=1)
    low_half = jnp.concatenate([sine_part, cosine], axis=1)
    return jnp.concatenate([top_half, low_half], axis=0).astype(jnp.bfloat16)

def channelize(samples, filter_taps, table):
    gate_count = samples.shape[0]
    folded = samples.astype(jnp.float32).reshape(gate_count, 2, TAPS, CHANNELS)
    filtered = lax.optimization_barrier(jnp.sum(folded * filter_taps, axis=2)).astype(jnp.bfloat16)
    flattened = filtered.reshape(gate_count, 2 * CHANNELS)
    spectra = jnp.dot(flattened.astype(jnp.float32), table.astype(jnp.float32), preferred_element_type=jnp.float32)
    return spectra.astype(jnp.bfloat16).reshape(gate_count, 2, BINS)

def compress(padded, range_code):
    gate_count = padded.shape[1] - 2 * CODE_REACH
    shape_out = (padded.shape[0], gate_count, padded.shape[3])
    real_sum = jnp.zeros(shape_out, jnp.float32)
    imag_sum = jnp.zeros(shape_out, jnp.float32)
    for offset in range(2 * CODE_REACH + 1):
        window = lax.slice_in_dim(padded, offset, offset + gate_count, axis=1).astype(jnp.float32)
        real_sum = real_sum + range_code[0, offset] * window[:, :, 0] - range_code[1, offset] * window[:, :, 1]
        imag_sum = imag_sum + range_code[0, offset] * window[:, :, 1] + range_code[1, offset] * window[:, :, 0]
    return jnp.stack([real_sum, imag_sum], axis=2).astype(jnp.bfloat16)

def local_gram(masked):
    real_rows = masked[:, :, 0]
    imag_rows = masked[:, :, 1]
    top_rows = jnp.concatenate([real_rows, imag_rows], axis=2)
    low_rows = jnp.concatenate([-imag_rows, real_rows], axis=2)
    stacked = jnp.concatenate([top_rows, low_rows], axis=1).astype(jnp.float32)
    return jnp.einsum('bri,brj->bij', stacked, stacked, precision=lax.Precision.HIGHEST)

def steering_table(steer_rows):
    element = jnp.arange(ELEMENTS, dtype=jnp.int32)
    turn_count = jnp.mod(element[None, :, None] * (2 * steer_rows[:, None, :] - ELEMENTS), 2 * ELEMENTS).astype(jnp.float32)
    phases = turn_count * (math.pi / ELEMENTS)
    return jnp.concatenate([jnp.cos(phases), jnp.sin(phases)], axis=1)

def solve_all(factor, steering):
    return jax.vmap(lambda lower_part, target: jax.scipy.linalg.cho_solve((lower_part, True), target))(factor, steering)

def beam_output(compressed, weights, steering):
    response = lax.optimization_barrier(jnp.sum(steering * weights, axis=1))
    signal = compressed.astype(jnp.float32)
    weight_real = weights[:, :ELEMENTS]
    weight_imag = weights[:, ELEMENTS:]
    highest = lax.Precision.HIGHEST
    out_real = jnp.einsum('bik,bgi->bkg', weight_real, signal[:, :, 0], precision=highest) + jnp.einsum('bik,bgi->bkg', weight_imag, signal[:, :, 1], precision=highest)
    out_imag = jnp.einsum('bik,bgi->bkg', weight_real, signal[:, :, 1], precision=highest) - jnp.einsum('bik,bgi->bkg', weight_imag, signal[:, :, 0], precision=highest)
    return jnp.stack([out_real, out_imag], axis=0) / jnp.sqrt(response)[None, :, :, None]

def adapt_one(inputs):
    compressed, mask_row, steer_row = inputs
    compressed = compressed[None]
    masked = compressed * mask_row.astype(jnp.bfloat16)[None, :, None, None]
    identity = jnp.eye(2 * ELEMENTS, dtype=jnp.float32)
    gram = local_gram(masked) / GATES + loading_level * identity
    factor = jnp.linalg.cholesky(gram)
    steering = steering_table(steer_row[None])
    weights = solve_all(factor, steering)
    return beam_output(compressed, weights, steering)[:, 0]

def reference(raw_samples, filter_taps, range_code, train_mask, steer_index):
    table = dft_table(BINS)
    per_element = lax.map(lambda samples: channelize(samples, filter_taps, table), raw_samples)
    spectra = jnp.transpose(per_element, (3, 1, 2, 0))
    padded = jnp.pad(spectra, ((0, 0), (CODE_REACH, CODE_REACH), (0, 0), (0, 0)))
    compressed = compress(padded, range_code)
    outputs = lax.map(adapt_one, (compressed, train_mask, steer_index))
    return jnp.transpose(outputs, (1, 0, 2, 3))
```

```python
import math

import jax
import jax.numpy as jnp
import numpy as np
from jax import lax
from jax.experimental import pallas as pl
from jax.experimental.pallas import tpu as pltpu
from jax.sharding import PartitionSpec as P

CHANNELS = 512
TAPS = 8
CODE_REACH = 3
LOADING = 0.25
BLOCK = 32
STEP = 4
LANES = 128
HEAD = 8
MASK_ROWS = 8

HIGHEST = lax.Precision.HIGHEST


def dft_columns(bin_total):
    mode = np.arange(CHANNELS, dtype=np.int64)[:, None]
    turn = (mode * np.arange(bin_total, dtype=np.int64)[None, :]) % CHANNELS
    phases = turn.astype(np.float32) * np.float32(2.0 * math.pi / CHANNELS)
    scale = np.float32(math.sqrt(CHANNELS))
    both = np.concatenate([np.cos(phases) / scale, np.sin(phases) / scale], axis=1)
    return jnp.asarray(both, jnp.bfloat16)


def mm(a, b, dims, precision=HIGHEST):
    return lax.dot_general(
        a, b, (dims, ((), ())), precision=precision, preferred_element_type=jnp.float32
    )


NN = ((1,), (0,))
TN = ((0,), (0,))
NT = ((1,), (1,))


def eliminate(work, turned):
    rows = lax.broadcasted_iota(jnp.int32, work.shape, 0)
    scale = jnp.zeros_like(work)
    for base in range(0, BLOCK, STEP):
        col_re = [jnp.broadcast_to(work[:, base + t : base + t + 1], work.shape) for t in range(STEP)]
        col_im = [
            jnp.broadcast_to(work[:, BLOCK + base + t : BLOCK + base + t + 1], work.shape)
            for t in range(STEP)
        ]
        for t in range(STEP):
            j = base + t
            pivot = jnp.broadcast_to(col_re[t][j : j + 1], (8, LANES))
            inverse = jnp.concatenate([1.0 / pivot] * (BLOCK // 8), axis=0)
            below = rows > j
            m_re = jnp.where(below, col_re[t] * inverse, 0.0)
            m_im = jnp.where(below, col_im[t] * inverse, 0.0)
            for u in range(t + 1, STEP):
                e_re = jnp.broadcast_to(col_re[u][j : j + 1], work.shape)
                e_im = jnp.broadcast_to(col_im[u][j : j + 1], work.shape)
                col_re[u], col_im[u] = (
                    col_re[u] - m_re * e_re + m_im * e_im,
                    col_im[u] - m_re * e_im - m_im * e_re,
                )
            row = jnp.broadcast_to(work[j : j + 1], work.shape)
            row_turned = jnp.broadcast_to(turned[j : j + 1], work.shape)
            work, turned = (
                work - m_re * row - m_im * row_turned,
                turned - m_re * row_turned + m_im * row,
            )
            scale = jnp.where(rows == j, inverse, scale)
    scale = jnp.sqrt(scale)
    return work * scale, turned * scale


def adapt_kernel(
    place_ref,
    code_ref,
    chunks_ref,
    rhs_re_ref,
    rhs_im_ref,
    own_ref,
    other_ref,
    sig_re,
    sig_im,
    x_re,
    x_im,
    train,
    mat_re,
    mat_im,
    emb_ref,
    wts_ref,
):
    chunk_count, _, _, elements = chunks_ref.shape
    gate_dev = (chunks_ref.shape[2] - MASK_ROWS) // 2
    gates = chunk_count * gate_dev
    width = elements + LANES
    zero = jnp.zeros((HEAD, elements), jnp.float32)
    for ref in (sig_re, sig_im):
        ref[0:HEAD] = zero
        ref[HEAD + gates : 2 * HEAD + gates] = zero
    for c in range(chunk_count):
        chunk = chunks_ref[c, 0].astype(jnp.float32)
        at = HEAD + c * gate_dev
        sig_re[at : at + gate_dev] = chunk[:gate_dev]
        sig_im[at : at + gate_dev] = chunk[gate_dev : 2 * gate_dev]

    diagonal = lax.broadcasted_iota(jnp.int32, (gate_dev, LANES), 0) == lax.broadcasted_iota(
        jnp.int32, (gate_dev, LANES), 1
    )
    for c in range(chunk_count):
        at = c * gate_dev
        real = jnp.zeros((gate_dev, elements), jnp.float32)
        imag = jnp.zeros((gate_dev, elements), jnp.float32)
        for t in range(2 * CODE_REACH + 1):
            start = HEAD + at + t - CODE_REACH
            w_re = sig_re[start : start + gate_dev]
            w_im = sig_im[start : start + gate_dev]
            c_re, c_im = code_ref[0, t], code_ref[1, t]
            real = real + c_re * w_re - c_im * w_im
            imag = imag + c_re * w_im + c_im * w_re
        real = real.astype(jnp.bfloat16).astype(jnp.float32)
        imag = imag.astype(jnp.bfloat16).astype(jnp.float32)
        x_re[at : at + gate_dev] = real
        x_im[at : at + gate_dev] = imag
        mask_row = chunks_ref[c, 0, 2 * gate_dev : 2 * gate_dev + 8, :LANES].astype(jnp.float32)[:1]
        mask = jnp.sum(jnp.where(diagonal, mask_row, 0.0), axis=1, keepdims=True)
        train[at : at + gate_dev, :elements] = (real * mask).astype(jnp.bfloat16)
        train[at : at + gate_dev, elements:] = (imag * mask).astype(jnp.bfloat16)

    a, b = train[:, :elements], train[:, elements:]
    left = jnp.concatenate([a, b], axis=0)
    right = jnp.concatenate([b, -a], axis=0)
    share = 1.0 / gates
    gram_re = mm(left, left, TN, None)
    gram_im = mm(right, left, TN, None)
    corner = lax.broadcasted_iota(jnp.int32, (elements, elements), 0) == lax.broadcasted_iota(
        jnp.int32, (elements, elements), 1
    )
    mat_re[:, :elements] = gram_re * share + jnp.where(corner, LOADING, 0.0)
    mat_im[:, :elements] = gram_im * share
    mat_re[:, elements:] = rhs_re_ref[...]
    mat_im[:, elements:] = rhs_im_ref[...]

    lane = lax.broadcasted_iota(jnp.int32, (BLOCK, BLOCK), 1)
    unit = jnp.where(lax.broadcasted_iota(jnp.int32, (BLOCK, BLOCK), 0) == lane, 1.0, 0.0)
    blank = jnp.zeros((BLOCK, BLOCK), jnp.float32)
    steps = elements // BLOCK
    for k in range(steps):
        at = k * BLOCK
        d_re = mat_re[at : at + BLOCK, at : at + BLOCK]
        d_im = mat_im[at : at + BLOCK, at : at + BLOCK]
        work = jnp.concatenate([d_re, d_im, unit, blank], axis=1)
        turned = jnp.concatenate([-d_im, d_re, blank, unit], axis=1)
        work, turned = eliminate(work, turned)
        emb = jnp.concatenate([turned[:, 2 * BLOCK :], work[:, 2 * BLOCK :]], axis=0)
        emb_ref[k] = emb
        left_lane = at // LANES * LANES
        rows_re = mat_re[at : at + BLOCK, left_lane:]
        rows_im = mat_im[at : at + BLOCK, left_lane:]
        solved = mm(emb, jnp.concatenate([rows_im, rows_re], axis=0), NN)
        mat_re[at : at + BLOCK, left_lane:] = solved[:BLOCK]
        mat_im[at : at + BLOCK, left_lane:] = solved[BLOCK:]
        if k + 1 < steps:
            nxt = at + BLOCK
            cross = jnp.concatenate([solved[BLOCK:], -solved[:BLOCK]], axis=0)
            stem = solved[:, : elements - left_lane]
            upd_re = mm(stem, solved, TN)
            upd_im = mm(stem, cross, TN)
            mat_re[nxt:, left_lane:] = mat_re[nxt:, left_lane:] - upd_re[nxt - left_lane :]
            mat_im[nxt:, left_lane:] = mat_im[nxt:, left_lane:] - upd_im[nxt - left_lane :]

    wts_ref[...] = jnp.zeros_like(wts_ref)
    used = lax.broadcasted_iota(jnp.int32, (BLOCK, LANES), 1) < 4
    for k in reversed(range(steps)):
        at = k * BLOCK
        v_re = mat_re[at : at + BLOCK, elements:]
        v_im = mat_im[at : at + BLOCK, elements:]
        if k + 1 < steps:
            first = (at + BLOCK) // LANES * LANES
            r_re = mat_re[at : at + BLOCK, first:elements]
            r_im = mat_im[at : at + BLOCK, first:elements]
            prod = mm(jnp.concatenate([r_re, r_im], axis=0), wts_ref[first:], NN)
            top, low = prod[:BLOCK], prod[BLOCK:]
            v_re = v_re - top + pltpu.roll(low, 64, 1)
            v_im = v_im - low - pltpu.roll(top, 64, 1)
        v = jnp.concatenate([jnp.where(used, v_re, 0.0), jnp.where(used, v_im, 0.0)], axis=0)
        w = mm(emb_ref[k], v, TN)
        wts_ref[at : at + BLOCK] = w[BLOCK:] + pltpu.roll(w[:BLOCK], 64, 1)

    wts = wts_ref[...]
    paired = rhs_re_ref[...] + pltpu.roll(rhs_im_ref[...], 64, 1)
    half = jnp.sum(paired * wts, axis=0, keepdims=True)
    response = half + pltpu.roll(half, 64, 1)
    wts = wts * jnp.where(response > 0.0, lax.rsqrt(response), 0.0)
    for ref, slot in ((own_ref, 1), (other_ref, 2)):
        at = pl.multiple_of(place_ref[slot] * gate_dev, 8)
        from_re = mm(wts, x_re[pl.ds(at, gate_dev)], ((0,), (1,)))
        from_im = mm(wts, x_im[pl.ds(at, gate_dev)], ((0,), (1,)))
        ref[0:8, :gate_dev] = from_re[0:8] + from_im[64:72]
        ref[8:16, :gate_dev] = from_im[0:8] - from_re[64:72]


def adapt(place, code, chunks, rhs_re, rhs_im):
    count, _, rows, elements = chunks.shape
    gate_dev = (rows - MASK_ROWS) // 2
    gates = count * gate_dev
    width = elements + LANES
    whole = lambda shape: pl.BlockSpec(shape, lambda i, p: (0,) * len(shape))
    f32 = jnp.float32
    return pl.pallas_call(
        adapt_kernel,
        grid_spec=pltpu.PrefetchScalarGridSpec(
            num_scalar_prefetch=1,
            grid=(1,),
            in_specs=[
                pl.BlockSpec(memory_space=pltpu.SMEM),
                pl.BlockSpec((count, 1, rows, elements), lambda i, p: (0, p[0], 0, 0)),
                whole((elements, LANES)),
                whole((elements, LANES)),
            ],
            out_specs=[whole((16, LANES)), whole((16, LANES))],
            scratch_shapes=[
                pltpu.VMEM((gates + 2 * HEAD, elements), f32),
                pltpu.VMEM((gates + 2 * HEAD, elements), f32),
                pltpu.VMEM((gates, elements), f32),
                pltpu.VMEM((gates, elements), f32),
                pltpu.VMEM((gates, 2 * elements), jnp.bfloat16),
                pltpu.VMEM((elements, width), f32),
                pltpu.VMEM((elements, width), f32),
                pltpu.VMEM((elements // BLOCK, 2 * BLOCK, 2 * BLOCK), f32),
                pltpu.VMEM((elements, LANES), f32),
            ],
        ),
        out_shape=[jax.ShapeDtypeStruct((16, LANES), f32)] * 2,
        name="adapt",
    )(place, code, chunks, rhs_re, rhs_im)


def steering_columns(steer_row, elements):
    element = jnp.arange(elements, dtype=jnp.int32)
    turn = jnp.mod(
        element[:, None] * (2 * steer_row[None, :] - elements), 2 * elements
    ).astype(jnp.float32)
    phases = turn * (math.pi / elements)
    pad = ((0, 0), (0, LANES - steer_row.shape[0]))
    return jnp.pad(jnp.cos(phases), pad), jnp.pad(jnp.sin(phases), pad)


def shards(raw_samples, filter_taps, range_code, train_mask, steer_index):
    elem_dev, gate_dev = raw_samples.shape[:2]
    bin_dev, beams = steer_index.shape
    dop_count, rng_count = lax.axis_size("dop"), lax.axis_size("rng")
    elements = elem_dev * dop_count
    bin_total = bin_dev * dop_count
    total = jnp.zeros((elem_dev, gate_dev, 2, CHANNELS), jnp.float32)
    for t in range(TAPS):
        piece = raw_samples[..., t * CHANNELS : (t + 1) * CHANNELS].astype(jnp.float32)
        total = total + piece * filter_taps[t]
    filtered = total.astype(jnp.bfloat16)
    rows = jnp.transpose(filtered, (2, 1, 0, 3)).reshape(2 * gate_dev * elem_dev, CHANNELS)
    parts = lax.dot_general(
        dft_columns(bin_total), rows, (((0,), (1,)), ((), ())), preferred_element_type=jnp.float32
    )
    cosine, sine = parts[:bin_total], parts[bin_total:]
    half = gate_dev * elem_dev
    spec_re = cosine[:, :half] + sine[:, half:]
    spec_im = cosine[:, half:] - sine[:, :half]
    spectra = jnp.concatenate([spec_re, spec_im], axis=1).astype(jnp.bfloat16)
    turned = lax.all_to_all(spectra, "dop", split_axis=0, concat_axis=0, tiled=True)
    turned = turned.reshape(dop_count, bin_dev, 2 * gate_dev, elem_dev)
    turned = jnp.transpose(turned, (1, 2, 0, 3)).reshape(bin_dev, 2 * gate_dev, elements)
    mask = jnp.pad(
        train_mask.astype(jnp.bfloat16)[:, None, :],
        ((0, 0), (0, MASK_ROWS - 1), (0, elements - gate_dev)),
    )
    chunk = jnp.concatenate([turned, mask], axis=1)
    chunks = lax.all_gather(chunk, "rng", axis=0, tiled=False)
    position = lax.axis_index("rng")
    core = position % bin_dev
    place = jnp.stack([core, position, position ^ 1]).astype(jnp.int32)
    steer_row = lax.dynamic_index_in_dim(steer_index, core, 0, keepdims=False)
    rhs_re, rhs_im = steering_columns(steer_row, elements)
    own, other = adapt(place, range_code, chunks, rhs_re, rhs_im)
    swapped = lax.ppermute(other, "rng", [(i, i ^ 1) for i in range(rng_count)])
    trim = lambda x: x.reshape(2, 8, LANES)[:, :beams, :gate_dev]
    own, swapped = trim(own), trim(swapped)
    low = jnp.where(core == 0, own, swapped)
    high = jnp.where(core == 0, swapped, own)
    return jnp.stack([low, high], axis=1)


def solution(mesh):
    return jax.shard_map(
        shards,
        mesh=mesh,
        in_specs=(P("dop", "rng", None, None), P(), P(), P("dop", "rng"), P("dop", None)),
        out_specs=P(None, "dop", None, "rng"),
        check_vma=False,
    )
```

```python
import math

import jax
import jax.numpy as jnp
import numpy as np
from jax import lax
from jax.experimental import pallas as pl
from jax.experimental.pallas import tpu as pltpu
from jax.sharding import PartitionSpec as P

CHANNELS = 512
TAPS = 8
CODE_REACH = 3
LOADING = 0.25
BLOCK = 32
STEP = 4
LANES = 128
HEAD = 8
TILE = 96
MASK_ROWS = 8

HIGHEST = lax.Precision.HIGHEST


def dft_rows(bin_total):
    mode = np.arange(CHANNELS, dtype=np.int64)[None, :]
    turn = (mode * np.arange(bin_total, dtype=np.int64)[:, None]) % CHANNELS
    phases = turn.astype(np.float32) * np.float32(2.0 * math.pi / CHANNELS)
    scale = np.float32(math.sqrt(CHANNELS))
    both = np.concatenate([np.cos(phases) / scale, np.sin(phases) / scale], axis=0)
    return jnp.asarray(both, jnp.bfloat16)


def mm(a, b, dims, precision=HIGHEST):
    return lax.dot_general(
        a, b, (dims, ((), ())), precision=precision, preferred_element_type=jnp.float32
    )


NN = ((1,), (0,))
TN = ((0,), (0,))
NT = ((1,), (1,))


def eliminate(work, turned):
    rows = lax.broadcasted_iota(jnp.int32, work.shape, 0)
    scale = jnp.zeros_like(work)
    for base in range(0, BLOCK, STEP):
        col_re = [jnp.broadcast_to(work[:, base + t : base + t + 1], work.shape) for t in range(STEP)]
        col_im = [
            jnp.broadcast_to(work[:, BLOCK + base + t : BLOCK + base + t + 1], work.shape)
            for t in range(STEP)
        ]
        for t in range(STEP):
            j = base + t
            pivot = jnp.broadcast_to(col_re[t][j : j + 1], (8, LANES))
            inverse = jnp.concatenate([1.0 / pivot] * (BLOCK // 8), axis=0)
            below = rows > j
            m_re = jnp.where(below, col_re[t] * inverse, 0.0)
            m_im = jnp.where(below, col_im[t] * inverse, 0.0)
            for u in range(t + 1, STEP):
                e_re = jnp.broadcast_to(col_re[u][j : j + 1], work.shape)
                e_im = jnp.broadcast_to(col_im[u][j : j + 1], work.shape)
                col_re[u], col_im[u] = (
                    col_re[u] - m_re * e_re + m_im * e_im,
                    col_im[u] - m_re * e_im - m_im * e_re,
                )
            row = jnp.broadcast_to(work[j : j + 1], work.shape)
            row_turned = jnp.broadcast_to(turned[j : j + 1], work.shape)
            work, turned = (
                work - m_re * row - m_im * row_turned,
                turned - m_re * row_turned + m_im * row,
            )
            scale = jnp.where(rows == j, inverse, scale)
    return work * jnp.sqrt(scale)


def split3(x):
    high = x.astype(jnp.bfloat16)
    rest = x - high.astype(jnp.float32)
    mid = rest.astype(jnp.bfloat16)
    low = (rest - mid.astype(jnp.float32)).astype(jnp.bfloat16)
    return high, mid, low


def dot6(left, right):
    high, mid, low = left
    count = high.shape[0]
    first = mm(jnp.concatenate([high, mid, low], axis=0), right[0], NN, None)
    second = mm(jnp.concatenate([high, mid], axis=0), right[1], NN, None)
    third = mm(high, right[2], NN, None)
    small = first[2 * count :] + second[count:] + third
    return first[:count] + (first[count : 2 * count] + second[:count] + small)


def stack_turned(x, elements, sign):
    lane = lax.broadcasted_iota(jnp.int32, (x.shape[0], LANES), 1)
    tail = pltpu.roll(x[:, 2 * elements :], 64, 1)
    tail = jnp.where((lane < 64) == (sign > 0), -tail, tail)
    out = []
    for whole, end in zip(split3(x), split3(tail)):
        real, imag = whole[:, :elements], whole[:, elements : 2 * elements]
        real, imag = (-imag, real) if sign > 0 else (imag, -real)
        out.append(jnp.concatenate([whole, jnp.concatenate([real, imag, end], axis=1)], axis=0))
    return out


def adapt_kernel(
    place_ref,
    code_ref,
    chunks_ref,
    steer_re_ref,
    steer_im_ref,
    own_ref,
    other_ref,
    sig_re,
    sig_im,
    x_re,
    x_im,
    train,
    mat,
    v_high,
    v_mid,
    v_low,
    s_high,
    s_mid,
    s_low,
):
    chunk_count, _, _, elements = chunks_ref.shape
    gate_dev = (chunks_ref.shape[2] - MASK_ROWS) // 2
    gates = chunk_count * gate_dev
    f32, bf16 = jnp.float32, jnp.bfloat16
    for ref in (sig_re, sig_im):
        ref[0:HEAD] = jnp.zeros((HEAD, elements), f32)
        ref[HEAD + gates :] = jnp.zeros((ref.shape[0] - HEAD - gates, elements), f32)
    diagonal = lax.broadcasted_iota(jnp.int32, (gate_dev, LANES), 0) == lax.broadcasted_iota(
        jnp.int32, (gate_dev, LANES), 1
    )
    masks = []
    for c in range(chunk_count):
        chunk = chunks_ref[c, 0].astype(f32)
        at = HEAD + c * gate_dev
        sig_re[at : at + gate_dev] = chunk[:gate_dev]
        sig_im[at : at + gate_dev] = chunk[gate_dev : 2 * gate_dev]
        mask_row = chunk[2 * gate_dev : 2 * gate_dev + 1, :LANES]
        masks.append(jnp.sum(jnp.where(diagonal, mask_row, 0.0), axis=1, keepdims=True))

    tap = (
        lax.broadcasted_iota(jnp.int32, (TILE, LANES), 1)
        - lax.broadcasted_iota(jnp.int32, (TILE, LANES), 0)
        - (HEAD - CODE_REACH)
    )
    band_re = jnp.zeros((TILE, LANES), f32)
    band_im = jnp.zeros((TILE, LANES), f32)
    for t in range(2 * CODE_REACH + 1):
        band_re = jnp.where(tap == t, code_ref[0, t], band_re)
        band_im = jnp.where(tap == t, code_ref[1, t], band_im)
    band = jnp.concatenate(
        [
            jnp.concatenate([band_re, -band_im], axis=1),
            jnp.concatenate([band_im, band_re], axis=1),
        ],
        axis=0,
    )
    bands = split3(band)
    for c in range(gates // TILE):
        at = c * TILE
        window = jnp.concatenate(
            [sig_re[at : at + LANES].astype(bf16), sig_im[at : at + LANES].astype(bf16)], axis=0
        )
        high, mid, low = (mm(part, window, NN, None) for part in bands)
        both = (high + (mid + low)).astype(bf16).astype(f32)
        real, imag = both[:TILE], both[TILE:]
        x_re[at : at + TILE] = real
        x_im[at : at + TILE] = imag
        per = TILE // gate_dev
        mask = jnp.concatenate(masks[c * per : (c + 1) * per], axis=0)
        train[at : at + TILE, :elements] = (real * mask).astype(bf16)
        train[at : at + TILE, elements:] = (imag * mask).astype(bf16)

    a, b = train[:, :elements], train[:, elements:]
    left = jnp.concatenate([a, b], axis=0)
    right = jnp.concatenate([jnp.concatenate([a, -b], axis=1), jnp.concatenate([b, a], axis=1)], axis=0)
    gram = mm(left, right, TN, None) * (1.0 / gates)
    corner = lax.broadcasted_iota(jnp.int32, (elements, elements), 0) == lax.broadcasted_iota(
        jnp.int32, (elements, elements), 1
    )
    mat[:, :elements] = gram[:, :elements] + jnp.where(corner, LOADING, 0.0)
    mat[:, elements : 2 * elements] = gram[:, elements:]

    spare = jnp.zeros((64 - 8 - 2 * gate_dev, elements), f32)
    sides = []
    for steer_ref, ref in ((steer_re_ref, x_re), (steer_im_ref, x_im)):
        sides.append(steer_ref[...])
        for slot in (1, 2):
            at = pl.multiple_of(place_ref[slot] * gate_dev, 8)
            sides.append(ref[pl.ds(at, gate_dev)])
        sides.append(spare)
    mat[:, 2 * elements :] = jnp.concatenate(sides, axis=0).T

    lane = lax.broadcasted_iota(jnp.int32, (BLOCK, BLOCK), 1)
    unit = jnp.where(lax.broadcasted_iota(jnp.int32, (BLOCK, BLOCK), 0) == lane, 1.0, 0.0)
    blank = jnp.zeros((BLOCK, BLOCK), f32)
    steps = elements // BLOCK
    acc = mat[0:BLOCK]
    for k in range(steps):
        at, nxt = k * BLOCK, (k + 1) * BLOCK
        seen = 2 * at
        d_re = acc[:, at:nxt]
        d_im = acc[:, elements + at : elements + nxt]
        panel = stack_turned(acc, elements, 1)
        if k + 1 < steps:
            later = mat[nxt : nxt + BLOCK]
            if k > 0:
                later = later - dot6(
                    [ref[nxt : nxt + BLOCK, :seen] for ref in (s_high, s_mid, s_low)],
                    [ref[:seen] for ref in (v_high, v_mid, v_low)],
                )
        work = jnp.concatenate([d_re, d_im, unit, blank], axis=1)
        turned = jnp.concatenate([-d_im, d_re, blank, unit], axis=1)
        work = eliminate(work, turned)
        solved = dot6(split3(work[:, 2 * BLOCK :]), panel)
        mat[at:nxt, 2 * elements :] = solved[:, 2 * elements :]
        if k + 1 < steps:
            trail = stack_turned(solved, elements, -1)
            first = nxt // LANES * LANES
            stem = jnp.concatenate(
                [solved[:, first:elements], solved[:, elements + first : 2 * elements]], axis=0
            ).T
            stems = split3(stem[nxt - first :])
            acc = later - dot6([part[:BLOCK] for part in stems], trail)
            for ref, part in zip((v_high, v_mid, v_low), trail):
                ref[seen : seen + 2 * BLOCK] = part
            for ref, part in zip((s_high, s_mid, s_low), stems):
                ref[nxt:, seen : seen + 2 * BLOCK] = part

    whitened = mat[:, 2 * elements :]
    inner = mm(whitened, whitened, TN)
    top, low = inner[0:8], pltpu.roll(inner[64:72], 64, 1)
    real = top + low
    imag = pltpu.roll(top - low, 64, 1)
    own_lane = lax.broadcasted_iota(jnp.int32, (8, LANES), 1) == lax.broadcasted_iota(
        jnp.int32, (8, LANES), 0
    )
    response = jnp.sum(jnp.where(own_lane, real, 0.0), axis=1, keepdims=True)
    factor = lax.rsqrt(jnp.where(response > 0.0, response, 1.0))
    both = jnp.concatenate([real * factor, imag * factor], axis=0)
    own_ref[...] = pltpu.roll(both, LANES - 8, 1)
    other_ref[...] = pltpu.roll(both, LANES - 8 - gate_dev, 1)


def adapt(place, code, chunks, steer_re, steer_im):
    count, _, rows, elements = chunks.shape
    gate_dev = (rows - MASK_ROWS) // 2
    gates = count * gate_dev
    width = 2 * elements + LANES
    whole = lambda shape: pl.BlockSpec(shape, lambda i, p: (0,) * len(shape))
    f32, bf16 = jnp.float32, jnp.bfloat16
    return pl.pallas_call(
        adapt_kernel,
        grid_spec=pltpu.PrefetchScalarGridSpec(
            num_scalar_prefetch=1,
            grid=(1,),
            in_specs=[
                pl.BlockSpec(memory_space=pltpu.SMEM),
                pl.BlockSpec((count, 1, rows, elements), lambda i, p: (0, p[0], 0, 0)),
                whole((8, elements)),
                whole((8, elements)),
            ],
            out_specs=[whole((16, LANES)), whole((16, LANES))],
            scratch_shapes=[
                pltpu.VMEM((gates - TILE + LANES + HEAD, elements), f32),
                pltpu.VMEM((gates - TILE + LANES + HEAD, elements), f32),
                pltpu.VMEM((gates, elements), f32),
                pltpu.VMEM((gates, elements), f32),
                pltpu.VMEM((gates, 2 * elements), bf16),
                pltpu.VMEM((elements, width), f32),
            ]
            + [pltpu.VMEM((2 * elements, width), bf16)] * 3
            + [pltpu.VMEM((elements, 2 * elements), bf16)] * 3,
        ),
        out_shape=[jax.ShapeDtypeStruct((16, LANES), f32)] * 2,
        name="adapt",
    )(place, code, chunks, steer_re, steer_im)


def channel_kernel(raw_ref, taps_ref, table_ref, out_ref, filtered):
    step = pl.program_id(0)
    elem_dev = pl.num_programs(0)
    rows = out_ref.shape[1] // 2
    gate_dev = rows // 8
    weights = [taps_ref[t] for t in range(TAPS)]
    for g in range(gate_dev):
        at = g * 8 * TAPS
        piece = raw_ref[at : at + 8 * TAPS].astype(jnp.float32)
        total = piece[0:8] * weights[0]
        for t in range(1, TAPS):
            total = total + piece[8 * t : 8 * t + 8] * weights[t]
        to = pl.multiple_of((g * elem_dev + step) * 8, 8)
        filtered[pl.ds(to, 8)] = total.astype(jnp.bfloat16).astype(jnp.float32)

    @pl.when(step == elem_dev - 1)
    def _():
        sums = []
        for r in range(2):
            rows_r = jnp.concatenate(
                [filtered[pl.ds(2 * j + r, rows, stride=8)] for j in range(4)], axis=1
            ).astype(jnp.bfloat16)
            sums.append(mm(table_ref[...], rows_r, NT, None))
        half = out_ref.shape[0]
        re = sums[0][:half] + sums[1][half:]
        im = sums[1][:half] - sums[0][half:]
        out_ref[...] = jnp.concatenate([re, im], axis=1).astype(jnp.bfloat16)


def channelize(raw_samples, filter_taps, bin_total):
    elem_dev, gate_dev = raw_samples.shape[:2]
    tiles = CHANNELS // LANES
    flat = raw_samples.reshape(elem_dev, gate_dev, 2, TAPS * tiles, LANES)
    flat = jnp.transpose(flat, (0, 1, 3, 2, 4)).reshape(-1, LANES)
    taps = jnp.repeat(filter_taps.reshape(TAPS, tiles, 1, LANES), 2, axis=2).reshape(TAPS, 8, LANES)
    rows = gate_dev * elem_dev
    return pl.pallas_call(
        channel_kernel,
        grid=(elem_dev,),
        in_specs=[
            pl.BlockSpec((gate_dev * TAPS * tiles * 2, LANES), lambda e: (e, 0)),
            pl.BlockSpec((TAPS, 8, LANES), lambda e: (0, 0, 0)),
            pl.BlockSpec((2 * bin_total, CHANNELS), lambda e: (0, 0)),
        ],
        out_specs=pl.BlockSpec((bin_total, 2 * rows), lambda e: (0, 0)),
        out_shape=jax.ShapeDtypeStruct((bin_total, 2 * rows), jnp.bfloat16),
        scratch_shapes=[pltpu.VMEM((rows * 8, LANES), jnp.float32)],
        name="channelize",
    )(flat, taps, dft_rows(bin_total))


def steering_rows(steer_row, elements):
    element = jnp.arange(elements, dtype=jnp.int32)
    turn = jnp.mod(
        element[None, :] * (2 * steer_row[:, None] - elements), 2 * elements
    ).astype(jnp.float32)
    phases = turn * (math.pi / elements)
    pad = ((0, 8 - steer_row.shape[0]), (0, 0))
    return jnp.pad(jnp.cos(phases), pad), jnp.pad(jnp.sin(phases), pad)


def shards(raw_samples, filter_taps, range_code, train_mask, steer_index):
    elem_dev, gate_dev = raw_samples.shape[:2]
    bin_dev, beams = steer_index.shape
    dop_count, rng_count = lax.axis_size("dop"), lax.axis_size("rng")
    elements = elem_dev * dop_count
    bin_total = bin_dev * dop_count
    spectra = channelize(raw_samples, filter_taps, bin_total)
    turned = lax.all_to_all(spectra, "dop", split_axis=0, concat_axis=0, tiled=True)
    turned = turned.reshape(dop_count, bin_dev, 2 * gate_dev, elem_dev)
    turned = jnp.transpose(turned, (1, 2, 0, 3)).reshape(bin_dev, 2 * gate_dev, elements)
    mask = jnp.pad(
        train_mask.astype(jnp.bfloat16)[:, None, :],
        ((0, 0), (0, MASK_ROWS - 1), (0, elements - gate_dev)),
    )
    chunk = jnp.concatenate([turned, mask], axis=1)
    chunks = lax.all_gather(chunk, "rng", axis=0, tiled=False)
    position = lax.axis_index("rng")
    core = position % bin_dev
    place = jnp.stack([core, position, position ^ 1]).astype(jnp.int32)
    steer_row = lax.dynamic_index_in_dim(steer_index, core, 0, keepdims=False)
    steer_re, steer_im = steering_rows(steer_row, elements)
    own, other = adapt(place, range_code, chunks, steer_re, steer_im)
    swapped = lax.ppermute(other, "rng", [(i, i ^ 1) for i in range(rng_count)])
    trim = lambda x: x.reshape(2, 8, LANES)[:, :beams, :gate_dev]
    own, swapped = trim(own), trim(swapped)
    low = jnp.where(core == 0, own, swapped)
    high = jnp.where(core == 0, swapped, own)
    return jnp.stack([low, high], axis=1)


def solution(mesh):
    return jax.shard_map(
        shards,
        mesh=mesh,
        in_specs=(P("dop", "rng", None, None), P(), P(), P("dop", "rng"), P("dop", None)),
        out_specs=P(None, "dop", None, "rng"),
        check_vma=False,
    )
```

```python
import math

import jax
import jax.numpy as jnp
import numpy as np
from jax import lax
from jax.experimental import pallas as pl
from jax.experimental.pallas import tpu as pltpu
from jax.sharding import PartitionSpec as P

CHANNELS = 512
TAPS = 8
CODE_REACH = 3
LOADING = 0.25
BLOCK = 32
STEP = 8
LANES = 128
HEAD = 8
TILE = 96
MASK_ROWS = 8

HIGHEST = lax.Precision.HIGHEST


def dft_rows(bin_total):
    mode = np.arange(CHANNELS, dtype=np.int64)[None, :]
    turn = (mode * np.arange(bin_total, dtype=np.int64)[:, None]) % CHANNELS
    phases = turn.astype(np.float32) * np.float32(2.0 * math.pi / CHANNELS)
    scale = np.float32(math.sqrt(CHANNELS))
    both = np.concatenate([np.cos(phases) / scale, np.sin(phases) / scale], axis=0)
    return jnp.asarray(both, jnp.bfloat16)


def mm(a, b, dims, precision=HIGHEST):
    return lax.dot_general(
        a, b, (dims, ((), ())), precision=precision, preferred_element_type=jnp.float32
    )


NN = ((1,), (0,))
TN = ((0,), (0,))
NT = ((1,), (1,))


def eliminate(work):
    count = BLOCK // 8
    w = [work[8 * g : 8 * g + 8] for g in range(count)]
    rows = lax.broadcasted_iota(jnp.int32, (8, LANES), 0)
    even = lax.broadcasted_iota(jnp.int32, (8, LANES), 1) // BLOCK % 2 == 0
    scale = [jnp.zeros((8, LANES), jnp.float32)] * count
    spread = lambda x: jnp.broadcast_to(x, (8, LANES))
    for base in range(0, BLOCK, STEP):
        head = base // 8
        live = range(head, count)
        columns = lambda first: [
            {g: spread(w[g][:, first + t : first + t + 1]) for g in live} for t in range(STEP)
        ]
        col_re, col_im = columns(base), columns(BLOCK + base)
        turned = jnp.where(
            even, -pltpu.roll(w[head], LANES - BLOCK, 1), pltpu.roll(w[head], BLOCK, 1)
        )
        for t in range(STEP):
            r = (base + t) % 8
            at = slice(r, r + 1)
            inverse = 1.0 / spread(col_re[t][head][at])
            scale[head] = jnp.where(rows == r, inverse, scale[head])
            m_re = {g: col_re[t][g] * inverse for g in live}
            m_im = {g: col_im[t][g] * inverse for g in live}
            m_re[head] = jnp.where(rows > r, m_re[head], 0.0)
            m_im[head] = jnp.where(rows > r, m_im[head], 0.0)
            below = [g for g in live if g > head or r < 7]
            for u in range(t + 1, STEP):
                e_re, e_im = spread(col_re[u][head][at]), spread(col_im[u][head][at])
                for g in below:
                    col_re[u][g], col_im[u][g] = (
                        col_re[u][g] - (m_re[g] * e_re - m_im[g] * e_im),
                        col_im[u][g] - (m_re[g] * e_im + m_im[g] * e_re),
                    )
            row, row_turned = spread(w[head][at]), spread(turned[at])
            if r < 7:
                turned = turned - (m_re[head] * row_turned - m_im[head] * row)
            for g in below:
                w[g] = w[g] - (m_re[g] * row + m_im[g] * row_turned)
    return jnp.concatenate(w, axis=0) * jnp.sqrt(jnp.concatenate(scale, axis=0))


def split3(x):
    high = x.astype(jnp.bfloat16)
    rest = x - high.astype(jnp.float32)
    mid = rest.astype(jnp.bfloat16)
    low = (rest - mid.astype(jnp.float32)).astype(jnp.bfloat16)
    return high, mid, low


def dot6(left, right):
    high, mid, low = left
    count = high.shape[0]
    first = mm(jnp.concatenate([high, mid, low], axis=0), right[0], NN, None)
    second = mm(jnp.concatenate([high, mid], axis=0), right[1], NN, None)
    third = mm(high, right[2], NN, None)
    small = first[2 * count :] + second[count:] + third
    return first[:count] + (first[count : 2 * count] + second[:count] + small)


def stack_turned(x, elements, sign):
    lane = lax.broadcasted_iota(jnp.int32, (x.shape[0], LANES), 1)
    tail = pltpu.roll(x[:, 2 * elements :], 64, 1)
    tail = jnp.where((lane < 64) == (sign > 0), -tail, tail)
    out = []
    for whole, end in zip(split3(x), split3(tail)):
        real, imag = whole[:, :elements], whole[:, elements : 2 * elements]
        real, imag = (-imag, real) if sign > 0 else (imag, -real)
        out.append(jnp.concatenate([whole, jnp.concatenate([real, imag, end], axis=1)], axis=0))
    return out


def adapt_kernel(
    place_ref,
    code_ref,
    chunks_ref,
    steer_re_ref,
    steer_im_ref,
    own_ref,
    other_ref,
    sig_re,
    sig_im,
    x_re,
    x_im,
    train,
    mat,
    v_high,
    v_mid,
    v_low,
    s_high,
    s_mid,
    s_low,
):
    chunk_count, _, _, elements = chunks_ref.shape
    gate_dev = (chunks_ref.shape[2] - MASK_ROWS) // 2
    gates = chunk_count * gate_dev
    f32, bf16 = jnp.float32, jnp.bfloat16
    for ref in (sig_re, sig_im):
        ref[0:HEAD] = jnp.zeros((HEAD, elements), f32)
        ref[HEAD + gates :] = jnp.zeros((ref.shape[0] - HEAD - gates, elements), f32)
    diagonal = lax.broadcasted_iota(jnp.int32, (gate_dev, LANES), 0) == lax.broadcasted_iota(
        jnp.int32, (gate_dev, LANES), 1
    )
    masks = []
    for c in range(chunk_count):
        chunk = chunks_ref[c, 0].astype(f32)
        at = HEAD + c * gate_dev
        sig_re[at : at + gate_dev] = chunk[:gate_dev]
        sig_im[at : at + gate_dev] = chunk[gate_dev : 2 * gate_dev]
        mask_row = chunk[2 * gate_dev : 2 * gate_dev + 1, :LANES]
        masks.append(jnp.sum(jnp.where(diagonal, mask_row, 0.0), axis=1, keepdims=True))

    tap = (
        lax.broadcasted_iota(jnp.int32, (TILE, LANES), 1)
        - lax.broadcasted_iota(jnp.int32, (TILE, LANES), 0)
        - (HEAD - CODE_REACH)
    )
    band_re = jnp.zeros((TILE, LANES), f32)
    band_im = jnp.zeros((TILE, LANES), f32)
    for t in range(2 * CODE_REACH + 1):
        band_re = jnp.where(tap == t, code_ref[0, t], band_re)
        band_im = jnp.where(tap == t, code_ref[1, t], band_im)
    band = jnp.concatenate(
        [
            jnp.concatenate([band_re, -band_im], axis=1),
            jnp.concatenate([band_im, band_re], axis=1),
        ],
        axis=0,
    )
    bands = split3(band)
    for c in range(gates // TILE):
        at = c * TILE
        window = jnp.concatenate(
            [sig_re[at : at + LANES].astype(bf16), sig_im[at : at + LANES].astype(bf16)], axis=0
        )
        high, mid, low = (mm(part, window, NN, None) for part in bands)
        both = (high + (mid + low)).astype(bf16).astype(f32)
        real, imag = both[:TILE], both[TILE:]
        x_re[at : at + TILE] = real
        x_im[at : at + TILE] = imag
        per = TILE // gate_dev
        mask = jnp.concatenate(masks[c * per : (c + 1) * per], axis=0)
        train[at : at + TILE, :elements] = (real * mask).astype(bf16)
        train[at : at + TILE, elements:] = (imag * mask).astype(bf16)

    a, b = train[:, :elements], train[:, elements:]
    left = jnp.concatenate([a, b], axis=0)
    right = jnp.concatenate([jnp.concatenate([a, -b], axis=1), jnp.concatenate([b, a], axis=1)], axis=0)
    gram = mm(left, right, TN, None) * (1.0 / gates)
    corner = lax.broadcasted_iota(jnp.int32, (elements, elements), 0) == lax.broadcasted_iota(
        jnp.int32, (elements, elements), 1
    )
    mat[:, :elements] = gram[:, :elements] + jnp.where(corner, LOADING, 0.0)
    mat[:, elements : 2 * elements] = gram[:, elements:]

    spare = jnp.zeros((64 - 8 - 2 * gate_dev, elements), f32)
    sides = []
    for steer_ref, ref in ((steer_re_ref, x_re), (steer_im_ref, x_im)):
        sides.append(steer_ref[...])
        for slot in (1, 2):
            at = pl.multiple_of(place_ref[slot] * gate_dev, 8)
            sides.append(ref[pl.ds(at, gate_dev)])
        sides.append(spare)
    mat[:, 2 * elements :] = jnp.concatenate(sides, axis=0).T

    lane = lax.broadcasted_iota(jnp.int32, (BLOCK, BLOCK), 1)
    unit = jnp.where(lax.broadcasted_iota(jnp.int32, (BLOCK, BLOCK), 0) == lane, 1.0, 0.0)
    blank = jnp.zeros((BLOCK, BLOCK), f32)
    steps = elements // BLOCK
    acc = mat[0:BLOCK]
    for k in range(steps):
        at, nxt = k * BLOCK, (k + 1) * BLOCK
        seen = 2 * at
        d_re = acc[:, at:nxt]
        d_im = acc[:, elements + at : elements + nxt]
        panel = stack_turned(acc, elements, 1)
        if k + 1 < steps:
            later = mat[nxt : nxt + BLOCK]
            if k > 0:
                later = later - dot6(
                    [ref[nxt : nxt + BLOCK, :seen] for ref in (s_high, s_mid, s_low)],
                    [ref[:seen] for ref in (v_high, v_mid, v_low)],
                )
        work = jnp.concatenate([d_re, d_im, unit, blank], axis=1)
        work = eliminate(work)
        solved = dot6(split3(work[:, 2 * BLOCK :]), panel)
        mat[at:nxt, 2 * elements :] = solved[:, 2 * elements :]
        if k + 1 < steps:
            trail = stack_turned(solved, elements, -1)
            first = nxt // LANES * LANES
            stem = jnp.concatenate(
                [solved[:, first:elements], solved[:, elements + first : 2 * elements]], axis=0
            ).T
            stems = split3(stem[nxt - first :])
            acc = later - dot6([part[:BLOCK] for part in stems], trail)
            for ref, part in zip((v_high, v_mid, v_low), trail):
                ref[seen : seen + 2 * BLOCK] = part
            for ref, part in zip((s_high, s_mid, s_low), stems):
                ref[nxt:, seen : seen + 2 * BLOCK] = part

    whitened = mat[:, 2 * elements :]
    inner = mm(whitened, whitened, TN)
    top, low = inner[0:8], pltpu.roll(inner[64:72], 64, 1)
    real = top + low
    imag = pltpu.roll(top - low, 64, 1)
    own_lane = lax.broadcasted_iota(jnp.int32, (8, LANES), 1) == lax.broadcasted_iota(
        jnp.int32, (8, LANES), 0
    )
    response = jnp.sum(jnp.where(own_lane, real, 0.0), axis=1, keepdims=True)
    factor = lax.rsqrt(jnp.where(response > 0.0, response, 1.0))
    both = jnp.concatenate([real * factor, imag * factor], axis=0)
    for ref, shift in ((own_ref, 8), (other_ref, 8 + gate_dev)):
        moved = pltpu.roll(both, LANES - shift, 1)
        for part in range(2):
            rows = moved[8 * part : 8 * part + 8]
            for b in range(2):
                ref[part, b] = jnp.where(place_ref[0] == b, rows, 0.0)


def adapt(place, code, chunks, steer_re, steer_im):
    count, _, rows, elements = chunks.shape
    gate_dev = (rows - MASK_ROWS) // 2
    gates = count * gate_dev
    width = 2 * elements + LANES
    whole = lambda shape: pl.BlockSpec(shape, lambda i, p: (0,) * len(shape))
    f32, bf16 = jnp.float32, jnp.bfloat16
    return pl.pallas_call(
        adapt_kernel,
        grid_spec=pltpu.PrefetchScalarGridSpec(
            num_scalar_prefetch=1,
            grid=(1,),
            in_specs=[
                pl.BlockSpec(memory_space=pltpu.SMEM),
                pl.BlockSpec((count, 1, rows, elements), lambda i, p: (0, p[0], 0, 0)),
                whole((8, elements)),
                whole((8, elements)),
            ],
            out_specs=[whole((2, 2, 8, LANES))] * 2,
            scratch_shapes=[
                pltpu.VMEM((gates - TILE + LANES + HEAD, elements), f32),
                pltpu.VMEM((gates - TILE + LANES + HEAD, elements), f32),
                pltpu.VMEM((gates, elements), f32),
                pltpu.VMEM((gates, elements), f32),
                pltpu.VMEM((gates, 2 * elements), bf16),
                pltpu.VMEM((elements, width), f32),
            ]
            + [pltpu.VMEM((2 * elements, width), bf16)] * 3
            + [pltpu.VMEM((elements, 2 * elements), bf16)] * 3,
        ),
        out_shape=[jax.ShapeDtypeStruct((2, 2, 8, LANES), f32)] * 2,
        name="adapt",
    )(place, code, chunks, steer_re, steer_im)


def channel_kernel(raw_ref, taps_ref, table_ref, out_ref, raw, filtered, arrived):
    elem_dev = arrived.shape[0]
    dests, bin_dev, lanes = out_ref.shape
    rows = lanes // 2
    gate_dev = rows // elem_dev
    per = gate_dev * 8 * TAPS
    copies = [
        pltpu.make_async_copy(
            raw_ref.at[pl.ds(e * per, per)], raw.at[pl.ds(e * per, per)], arrived.at[e]
        )
        for e in range(elem_dev)
    ]
    for copy in copies:
        copy.start()
    pair = lax.broadcasted_iota(jnp.int32, (8, LANES), 0) // 2
    weights = []
    for t in range(TAPS):
        weight = jnp.zeros((8, LANES), jnp.float32)
        for j in range(CHANNELS // LANES):
            piece = taps_ref[t : t + 1, j * LANES : (j + 1) * LANES]
            weight = jnp.where(pair == j, piece, weight)
        weights.append(weight)
    for e, copy in enumerate(copies):
        copy.wait()
        for g in range(gate_dev):
            at = e * per + g * 8 * TAPS
            piece = raw[at : at + 8 * TAPS].astype(jnp.float32)
            total = piece[0:8] * weights[0]
            for t in range(1, TAPS):
                total = total + piece[8 * t : 8 * t + 8] * weights[t]
            to = (g * elem_dev + e) * 8
            filtered[to : to + 8] = total.astype(jnp.bfloat16).astype(jnp.float32)
    sums = []
    for r in range(2):
        rows_r = jnp.concatenate(
            [filtered[pl.ds(2 * j + r, rows, stride=8)] for j in range(CHANNELS // LANES)], axis=1
        ).astype(jnp.bfloat16)
        sums.append(mm(table_ref[...], rows_r, NT, None))
    half = dests * bin_dev
    re = sums[0][:half] + sums[1][half:]
    im = sums[1][:half] - sums[0][half:]
    spectra = jnp.concatenate([re, im], axis=1).astype(jnp.bfloat16)
    for d in range(dests):
        out_ref[d] = spectra[bin_dev * d : bin_dev * (d + 1)]


def channelize(raw_samples, filter_taps, bin_dev, dop_count):
    elem_dev, gate_dev = raw_samples.shape[:2]
    tiles = CHANNELS // LANES
    flat = raw_samples.reshape(elem_dev, gate_dev, 2, TAPS * tiles, LANES)
    flat = jnp.transpose(flat, (0, 1, 3, 2, 4)).reshape(-1, LANES)
    rows = gate_dev * elem_dev
    return pl.pallas_call(
        channel_kernel,
        in_specs=[
            pl.BlockSpec(memory_space=pl.ANY),
            pl.BlockSpec(memory_space=pltpu.VMEM),
            pl.BlockSpec(memory_space=pltpu.VMEM),
        ],
        out_specs=pl.BlockSpec(memory_space=pltpu.VMEM),
        out_shape=jax.ShapeDtypeStruct((dop_count, bin_dev, 2 * rows), jnp.bfloat16),
        scratch_shapes=[
            pltpu.VMEM(flat.shape, jnp.bfloat16),
            pltpu.VMEM((rows * 8, LANES), jnp.float32),
            pltpu.SemaphoreType.DMA((elem_dev,)),
        ],
        name="channelize",
    )(flat, filter_taps, dft_rows(dop_count * bin_dev))


def steering_rows(steer_row, elements):
    element = jnp.arange(elements, dtype=jnp.int32)
    turn = jnp.mod(
        element[None, :] * (2 * steer_row[:, None] - elements), 2 * elements
    ).astype(jnp.float32)
    phases = turn * (math.pi / elements)
    pad = ((0, 8 - steer_row.shape[0]), (0, 0))
    return jnp.pad(jnp.cos(phases), pad), jnp.pad(jnp.sin(phases), pad)


def shards(raw_samples, filter_taps, range_code, train_mask, steer_index):
    elem_dev, gate_dev = raw_samples.shape[:2]
    bin_dev, beams = steer_index.shape
    dop_count, rng_count = lax.axis_size("dop"), lax.axis_size("rng")
    elements = elem_dev * dop_count
    spectra = channelize(raw_samples, filter_taps, bin_dev, dop_count)
    turned = lax.all_to_all(spectra, "dop", split_axis=0, concat_axis=0, tiled=True)
    turned = turned.reshape(dop_count, bin_dev, 2 * gate_dev, elem_dev)
    turned = jnp.transpose(turned, (1, 2, 0, 3)).reshape(bin_dev, 2 * gate_dev, elements)
    mask = jnp.pad(
        train_mask.astype(jnp.bfloat16)[:, None, :],
        ((0, 0), (0, MASK_ROWS - 1), (0, elements - gate_dev)),
    )
    chunk = jnp.concatenate([turned, mask], axis=1)
    chunks = lax.all_gather(chunk, "rng", axis=0, tiled=False)
    position = lax.axis_index("rng")
    core = position % bin_dev
    place = jnp.stack([core, position, position ^ 1]).astype(jnp.int32)
    steer_row = lax.dynamic_index_in_dim(steer_index, core, 0, keepdims=False)
    steer_re, steer_im = steering_rows(steer_row, elements)
    own, other = adapt(place, range_code, chunks, steer_re, steer_im)
    swapped = lax.ppermute(other, "rng", [(i, i ^ 1) for i in range(rng_count)])
    return (own + swapped)[:, :, :beams, :gate_dev]


def solution(mesh):
    return jax.shard_map(
        shards,
        mesh=mesh,
        in_specs=(P("dop", "rng", None, None), P(), P(), P("dop", "rng"), P("dop", None)),
        out_specs=P(None, "dop", None, "rng"),
        check_vma=False,
    )
```

```python
import math

import jax
import jax.numpy as jnp
import numpy as np
from jax import lax
from jax.experimental import pallas as pl
from jax.experimental.pallas import tpu as pltpu
from jax.sharding import PartitionSpec as P

CHANNELS = 512
TAPS = 8
CODE_REACH = 3
LOADING = 0.25
BLOCK = 32
STEP = 8
LANES = 128
HEAD = 8
TILE = 96
MASK_ROWS = 8

HIGHEST = lax.Precision.HIGHEST


def dft_rows(bin_total):
    mode = np.arange(CHANNELS, dtype=np.int64)[None, :]
    turn = (mode * np.arange(bin_total, dtype=np.int64)[:, None]) % CHANNELS
    phases = turn.astype(np.float32) * np.float32(2.0 * math.pi / CHANNELS)
    scale = np.float32(math.sqrt(CHANNELS))
    both = np.concatenate([np.cos(phases) / scale, np.sin(phases) / scale], axis=0)
    return jnp.asarray(both, jnp.bfloat16)


def mm(a, b, dims, precision=HIGHEST):
    return lax.dot_general(
        a, b, (dims, ((), ())), precision=precision, preferred_element_type=jnp.float32
    )


NN = ((1,), (0,))
TN = ((0,), (0,))
NT = ((1,), (1,))


def eliminate(work):
    count = BLOCK // 8
    w = [work[8 * g : 8 * g + 8] for g in range(count)]
    rows = lax.broadcasted_iota(jnp.int32, (8, LANES), 0)
    even = lax.broadcasted_iota(jnp.int32, (8, LANES), 1) // BLOCK % 2 == 0
    scale = [jnp.zeros((8, LANES), jnp.float32)] * count
    spread = lambda x: jnp.broadcast_to(x, (8, LANES))
    for base in range(0, BLOCK, STEP):
        head = base // 8
        live = range(head, count)
        col_re = [{} for _ in range(STEP)]
        col_im = [{} for _ in range(STEP)]
        for g in live:
            for t in range(STEP):
                c = 2 * BLOCK + base + t
                col_re[t][g] = spread(w[g][:, c : c + 1])
                col_im[t][g] = spread(w[g][:, BLOCK + c : BLOCK + c + 1])
        turned = jnp.where(
            even, -pltpu.roll(w[head], LANES - BLOCK, 1), pltpu.roll(w[head], BLOCK, 1)
        )
        for t in range(STEP):
            r = (base + t) % 8
            at = slice(r, r + 1)
            if t % 2 == 0:
                nxt = slice(r + 1, r + 2)
                first, second = spread(col_re[t][head][at]), spread(col_re[t + 1][head][nxt])
                x_re, x_im = spread(col_re[t + 1][head][at]), spread(col_im[t + 1][head][at])
                inverse = 1.0 / first
                following = first * (1.0 / (first * second - (x_re * x_re + x_im * x_im)))
            else:
                inverse = following
            scale[head] = jnp.where(rows == r, inverse, scale[head])
            m_re = {g: col_re[t][g] * inverse for g in live}
            m_im = {g: col_im[t][g] * inverse for g in live}
            m_re[head] = jnp.where(rows > r, m_re[head], 0.0)
            m_im[head] = jnp.where(rows > r, m_im[head], 0.0)
            below = [g for g in live if g > head or r < 7]
            for u in range(t + 1, STEP):
                e_re, e_im = spread(col_re[u][head][at]), spread(col_im[u][head][at])
                for g in below:
                    col_re[u][g], col_im[u][g] = (
                        col_re[u][g] - (m_re[g] * e_re - m_im[g] * e_im),
                        col_im[u][g] - (m_re[g] * e_im + m_im[g] * e_re),
                    )
            row, row_turned = spread(w[head][at]), spread(turned[at])
            if r < 7:
                turned = turned - (m_re[head] * row_turned - m_im[head] * row)
            for g in below:
                w[g] = w[g] - (m_re[g] * row + m_im[g] * row_turned)
    return jnp.concatenate(w, axis=0) * jnp.sqrt(jnp.concatenate(scale, axis=0))


def split3(x):
    high = x.astype(jnp.bfloat16)
    rest = x - high.astype(jnp.float32)
    mid = rest.astype(jnp.bfloat16)
    low = (rest - mid.astype(jnp.float32)).astype(jnp.bfloat16)
    return high, mid, low


def dot6(left, right):
    high, mid, low = left
    count = high.shape[0]
    first = mm(jnp.concatenate([high, mid, low], axis=0), right[0], NN, None)
    second = mm(jnp.concatenate([high, mid], axis=0), right[1], NN, None)
    third = mm(high, right[2], NN, None)
    small = first[2 * count :] + second[count:] + third
    return first[:count] + (first[count : 2 * count] + second[:count] + small)


def stack_turned(x, elements, sign):
    lane = lax.broadcasted_iota(jnp.int32, (x.shape[0], LANES), 1)
    tail = pltpu.roll(x[:, 2 * elements :], 64, 1)
    tail = jnp.where((lane < 64) == (sign > 0), -tail, tail)
    out = []
    for whole, end in zip(split3(x), split3(tail)):
        real, imag = whole[:, :elements], whole[:, elements : 2 * elements]
        real, imag = (-imag, real) if sign > 0 else (imag, -real)
        out.append(jnp.concatenate([whole, jnp.concatenate([real, imag, end], axis=1)], axis=0))
    return out


def adapt_kernel(
    place_ref,
    code_ref,
    chunks_ref,
    steer_re_ref,
    steer_im_ref,
    own_ref,
    other_ref,
    sig_re,
    sig_im,
    x_re,
    x_im,
    train,
    mat,
    v_high,
    v_mid,
    v_low,
    s_high,
    s_mid,
    s_low,
):
    chunk_count, _, _, elements = chunks_ref.shape
    _, bin_dev, beams, _ = own_ref.shape
    gate_dev = (chunks_ref.shape[2] - MASK_ROWS) // 2
    gates = chunk_count * gate_dev
    f32, bf16 = jnp.float32, jnp.bfloat16
    for ref in (sig_re, sig_im):
        ref[0:HEAD] = jnp.zeros((HEAD, elements), f32)
        ref[HEAD + gates :] = jnp.zeros((ref.shape[0] - HEAD - gates, elements), f32)
    diagonal = lax.broadcasted_iota(jnp.int32, (gate_dev, LANES), 0) == lax.broadcasted_iota(
        jnp.int32, (gate_dev, LANES), 1
    )
    masks = []
    for c in range(chunk_count):
        chunk = chunks_ref[c, 0].astype(f32)
        at = HEAD + c * gate_dev
        sig_re[at : at + gate_dev] = chunk[:gate_dev]
        sig_im[at : at + gate_dev] = chunk[gate_dev : 2 * gate_dev]
        mask_row = chunk[2 * gate_dev : 2 * gate_dev + 1, :LANES]
        masks.append(jnp.sum(jnp.where(diagonal, mask_row, 0.0), axis=1, keepdims=True))

    tap = (
        lax.broadcasted_iota(jnp.int32, (TILE, LANES), 1)
        - lax.broadcasted_iota(jnp.int32, (TILE, LANES), 0)
        - (HEAD - CODE_REACH)
    )
    band_re = jnp.zeros((TILE, LANES), f32)
    band_im = jnp.zeros((TILE, LANES), f32)
    for t in range(2 * CODE_REACH + 1):
        band_re = jnp.where(tap == t, code_ref[0, t], band_re)
        band_im = jnp.where(tap == t, code_ref[1, t], band_im)
    band = jnp.concatenate(
        [
            jnp.concatenate([band_re, -band_im], axis=1),
            jnp.concatenate([band_im, band_re], axis=1),
        ],
        axis=0,
    )
    bands = split3(band)
    for c in range(gates // TILE):
        at = c * TILE
        window = jnp.concatenate(
            [sig_re[at : at + LANES].astype(bf16), sig_im[at : at + LANES].astype(bf16)], axis=0
        )
        high, mid, low = (mm(part, window, NN, None) for part in bands)
        both = (high + (mid + low)).astype(bf16).astype(f32)
        real, imag = both[:TILE], both[TILE:]
        x_re[at : at + TILE] = real
        x_im[at : at + TILE] = imag
        per = TILE // gate_dev
        mask = jnp.concatenate(masks[c * per : (c + 1) * per], axis=0)
        train[at : at + TILE, :elements] = (real * mask).astype(bf16)
        train[at : at + TILE, elements:] = (imag * mask).astype(bf16)

    a, b = train[:, :elements], train[:, elements:]
    left = jnp.concatenate([a, b], axis=0)
    right = jnp.concatenate([jnp.concatenate([a, -b], axis=1), jnp.concatenate([b, a], axis=1)], axis=0)
    gram = mm(left, right, TN, None) * (1.0 / gates)
    corner = lax.broadcasted_iota(jnp.int32, (elements, elements), 0) == lax.broadcasted_iota(
        jnp.int32, (elements, elements), 1
    )
    mat[:, :elements] = gram[:, :elements] + jnp.where(corner, LOADING, 0.0)
    mat[:, elements : 2 * elements] = gram[:, elements:]

    spare = jnp.zeros((64 - 8 - 2 * gate_dev, elements), f32)
    sides = []
    for steer_ref, ref in ((steer_re_ref, x_re), (steer_im_ref, x_im)):
        sides.append(steer_ref[...])
        for slot in (1, 2):
            at = pl.multiple_of(place_ref[slot] * gate_dev, 8)
            sides.append(ref[pl.ds(at, gate_dev)])
        sides.append(spare)
    mat[:, 2 * elements :] = jnp.concatenate(sides, axis=0).T

    lane = lax.broadcasted_iota(jnp.int32, (BLOCK, BLOCK), 1)
    unit = jnp.where(lax.broadcasted_iota(jnp.int32, (BLOCK, BLOCK), 0) == lane, 1.0, 0.0)
    blank = jnp.zeros((BLOCK, BLOCK), f32)
    steps = elements // BLOCK
    acc = mat[0:BLOCK]
    for k in range(steps):
        at, nxt = k * BLOCK, (k + 1) * BLOCK
        seen = 2 * at
        d_re = acc[:, at:nxt]
        d_im = acc[:, elements + at : elements + nxt]
        panel = stack_turned(acc, elements, 1)
        if k + 1 < steps:
            later = mat[nxt : nxt + BLOCK]
            if k > 0:
                later = later - dot6(
                    [ref[nxt : nxt + BLOCK, :seen] for ref in (s_high, s_mid, s_low)],
                    [ref[:seen] for ref in (v_high, v_mid, v_low)],
                )
        work = jnp.concatenate([unit, blank, d_re, d_im], axis=1)
        work = eliminate(work)
        solved = dot6(split3(work[:, : 2 * BLOCK]), panel)
        mat[at:nxt, 2 * elements :] = solved[:, 2 * elements :]
        if k + 1 < steps:
            trail = stack_turned(solved, elements, -1)
            first = nxt // LANES * LANES
            stem = jnp.concatenate(
                [solved[:, first:elements], solved[:, elements + first : 2 * elements]], axis=0
            ).T
            stems = split3(stem[nxt - first :])
            acc = later - dot6([part[:BLOCK] for part in stems], trail)
            for ref, part in zip((v_high, v_mid, v_low), trail):
                ref[seen : seen + 2 * BLOCK] = part
            for ref, part in zip((s_high, s_mid, s_low), stems):
                ref[nxt:, seen : seen + 2 * BLOCK] = part

    whitened = mat[:, 2 * elements :]
    inner = mm(whitened, whitened, TN)
    top, low = inner[0:8], pltpu.roll(inner[64:72], 64, 1)
    real = top + low
    imag = pltpu.roll(top - low, 64, 1)
    own_lane = lax.broadcasted_iota(jnp.int32, (8, LANES), 1) == lax.broadcasted_iota(
        jnp.int32, (8, LANES), 0
    )
    response = jnp.sum(jnp.where(own_lane, real, 0.0), axis=1, keepdims=True)
    factor = lax.rsqrt(jnp.where(response > 0.0, response, 1.0))
    both = jnp.concatenate([real * factor, imag * factor], axis=0)
    for ref, shift in ((own_ref, 8), (other_ref, 8 + gate_dev)):
        moved = pltpu.roll(both, LANES - shift, 1)
        for part in range(2):
            rows = moved[8 * part : 8 * part + beams, :gate_dev]
            for b in range(bin_dev):
                ref[part, b] = jnp.where(place_ref[0] == b, rows, 0.0)


def adapt(place, code, chunks, steer_re, steer_im, beams):
    count, bin_dev, rows, elements = chunks.shape
    gate_dev = (rows - MASK_ROWS) // 2
    gates = count * gate_dev
    width = 2 * elements + LANES
    out = (2, bin_dev, beams, gate_dev)
    whole = lambda shape: pl.BlockSpec(shape, lambda i, p: (0,) * len(shape))
    f32, bf16 = jnp.float32, jnp.bfloat16
    return pl.pallas_call(
        adapt_kernel,
        grid_spec=pltpu.PrefetchScalarGridSpec(
            num_scalar_prefetch=1,
            grid=(1,),
            in_specs=[
                pl.BlockSpec(memory_space=pltpu.SMEM),
                pl.BlockSpec((count, 1, rows, elements), lambda i, p: (0, p[0], 0, 0)),
                whole((8, elements)),
                whole((8, elements)),
            ],
            out_specs=[whole(out)] * 2,
            scratch_shapes=[
                pltpu.VMEM((gates - TILE + LANES + HEAD, elements), f32),
                pltpu.VMEM((gates - TILE + LANES + HEAD, elements), f32),
                pltpu.VMEM((gates, elements), f32),
                pltpu.VMEM((gates, elements), f32),
                pltpu.VMEM((gates, 2 * elements), bf16),
                pltpu.VMEM((elements, width), f32),
            ]
            + [pltpu.VMEM((2 * elements, width), bf16)] * 3
            + [pltpu.VMEM((elements, 2 * elements), bf16)] * 3,
        ),
        out_shape=[jax.ShapeDtypeStruct(out, f32)] * 2,
        name="adapt",
    )(place, code, chunks, steer_re, steer_im)


def channel_kernel(raw_ref, taps_ref, table_ref, out_ref, raw, filtered, arrived):
    elem_dev = arrived.shape[0]
    dests, bin_dev, lanes = out_ref.shape
    rows = lanes // 2
    gate_dev = rows // elem_dev
    per = gate_dev * 8 * TAPS
    copies = [
        pltpu.make_async_copy(
            raw_ref.at[pl.ds(e * per, per)], raw.at[pl.ds(e * per, per)], arrived.at[e]
        )
        for e in range(elem_dev)
    ]
    for copy in copies:
        copy.start()
    pair = lax.broadcasted_iota(jnp.int32, (8, LANES), 0) // 2
    weights = []
    for t in range(TAPS):
        weight = jnp.zeros((8, LANES), jnp.float32)
        for j in range(CHANNELS // LANES):
            piece = taps_ref[t : t + 1, j * LANES : (j + 1) * LANES]
            weight = jnp.where(pair == j, piece, weight)
        weights.append(weight)
    for e, copy in enumerate(copies):
        copy.wait()
        for g in range(gate_dev):
            at = e * per + g * 8 * TAPS
            piece = raw[at : at + 8 * TAPS].astype(jnp.float32)
            total = piece[0:8] * weights[0]
            for t in range(1, TAPS):
                total = total + piece[8 * t : 8 * t + 8] * weights[t]
            to = (g * elem_dev + e) * 8
            filtered[to : to + 8] = total.astype(jnp.bfloat16).astype(jnp.float32)
    sums = []
    for r in range(2):
        rows_r = jnp.concatenate(
            [filtered[pl.ds(2 * j + r, rows, stride=8)] for j in range(CHANNELS // LANES)], axis=1
        ).astype(jnp.bfloat16)
        sums.append(mm(table_ref[...], rows_r, NT, None))
    half = dests * bin_dev
    re = sums[0][:half] + sums[1][half:]
    im = sums[1][:half] - sums[0][half:]
    spectra = jnp.concatenate([re, im], axis=1).astype(jnp.bfloat16)
    for d in range(dests):
        out_ref[d] = spectra[bin_dev * d : bin_dev * (d + 1)]


def channelize(raw_samples, filter_taps, bin_dev, dop_count):
    elem_dev, gate_dev = raw_samples.shape[:2]
    tiles = CHANNELS // LANES
    flat = raw_samples.reshape(elem_dev, gate_dev, 2, TAPS * tiles, LANES)
    flat = jnp.transpose(flat, (0, 1, 3, 2, 4)).reshape(-1, LANES)
    rows = gate_dev * elem_dev
    return pl.pallas_call(
        channel_kernel,
        in_specs=[
            pl.BlockSpec(memory_space=pl.ANY),
            pl.BlockSpec(memory_space=pltpu.VMEM),
            pl.BlockSpec(memory_space=pltpu.VMEM),
        ],
        out_specs=pl.BlockSpec(memory_space=pltpu.VMEM),
        out_shape=jax.ShapeDtypeStruct((dop_count, bin_dev, 2 * rows), jnp.bfloat16),
        scratch_shapes=[
            pltpu.VMEM(flat.shape, jnp.bfloat16),
            pltpu.VMEM((rows * 8, LANES), jnp.float32),
            pltpu.SemaphoreType.DMA((elem_dev,)),
        ],
        name="channelize",
    )(flat, filter_taps, dft_rows(dop_count * bin_dev))


def steering_rows(steer_row, elements):
    element = jnp.arange(elements, dtype=jnp.int32)
    turn = jnp.mod(
        element[None, :] * (2 * steer_row[:, None] - elements), 2 * elements
    ).astype(jnp.float32)
    phases = turn * (math.pi / elements)
    pad = ((0, 8 - steer_row.shape[0]), (0, 0))
    return jnp.pad(jnp.cos(phases), pad), jnp.pad(jnp.sin(phases), pad)


def shards(raw_samples, filter_taps, range_code, train_mask, steer_index):
    elem_dev, gate_dev = raw_samples.shape[:2]
    bin_dev, beams = steer_index.shape
    dop_count, rng_count = lax.axis_size("dop"), lax.axis_size("rng")
    elements = elem_dev * dop_count
    spectra = channelize(raw_samples, filter_taps, bin_dev, dop_count)
    turned = lax.all_to_all(spectra, "dop", split_axis=0, concat_axis=0, tiled=True)
    turned = turned.reshape(dop_count, bin_dev, 2 * gate_dev, elem_dev)
    turned = jnp.transpose(turned, (1, 2, 0, 3)).reshape(bin_dev, 2 * gate_dev, elements)
    mask = jnp.pad(
        train_mask.astype(jnp.bfloat16)[:, None, :],
        ((0, 0), (0, MASK_ROWS - 1), (0, elements - gate_dev)),
    )
    chunk = jnp.concatenate([turned, mask], axis=1)
    chunks = lax.all_gather(chunk, "rng", axis=0, tiled=False)
    position = lax.axis_index("rng")
    core = position % bin_dev
    place = jnp.stack([core, position, position ^ 1]).astype(jnp.int32)
    steer_row = lax.dynamic_index_in_dim(steer_index, core, 0, keepdims=False)
    steer_re, steer_im = steering_rows(steer_row, elements)
    own, other = adapt(place, range_code, chunks, steer_re, steer_im, beams)
    swapped = lax.ppermute(other, "rng", [(i, i ^ 1) for i in range(rng_count)])
    return own + swapped


def solution(mesh):
    return jax.shard_map(
        shards,
        mesh=mesh,
        in_specs=(P("dop", "rng", None, None), P(), P(), P("dop", "rng"), P("dop", None)),
        out_specs=P(None, "dop", None, "rng"),
        check_vma=False,
    )
```

```python
import math

import jax
import jax.numpy as jnp
import numpy as np
from jax import lax
from jax.experimental import pallas as pl
from jax.experimental.pallas import tpu as pltpu
from jax.sharding import PartitionSpec as P

CHANNELS = 512
TAPS = 8
CODE_REACH = 3
LOADING = 0.25
BLOCK = 32
STEP = 8
LANES = 128
HEAD = 8
TILE = 96
MASK_ROWS = 8

HIGHEST = lax.Precision.HIGHEST


def dft_rows(bin_total):
    mode = np.arange(CHANNELS, dtype=np.int64)[None, :]
    turn = (mode * np.arange(bin_total, dtype=np.int64)[:, None]) % CHANNELS
    phases = turn.astype(np.float32) * np.float32(2.0 * math.pi / CHANNELS)
    scale = np.float32(math.sqrt(CHANNELS))
    both = np.concatenate([np.cos(phases) / scale, np.sin(phases) / scale], axis=0)
    return jnp.asarray(both, jnp.bfloat16)


def mm(a, b, dims, precision=HIGHEST):
    return lax.dot_general(
        a, b, (dims, ((), ())), precision=precision, preferred_element_type=jnp.float32
    )


NN = ((1,), (0,))
TN = ((0,), (0,))
NT = ((1,), (1,))


def eliminate(work):
    count = BLOCK // 8
    w = [work[8 * g : 8 * g + 8] for g in range(count)]
    rows = lax.broadcasted_iota(jnp.int32, (8, LANES), 0)
    even = lax.broadcasted_iota(jnp.int32, (8, LANES), 1) // BLOCK % 2 == 0
    scale = [jnp.zeros((8, LANES), jnp.float32)] * count
    spread = lambda x: jnp.broadcast_to(x, (8, LANES))
    for base in range(0, BLOCK, STEP):
        head = base // 8
        live = range(head, count)
        col_re = [{} for _ in range(STEP)]
        col_im = [{} for _ in range(STEP)]
        for g in live:
            for t in range(STEP):
                c = 2 * BLOCK + base + t
                col_re[t][g] = spread(w[g][:, c : c + 1])
                col_im[t][g] = spread(w[g][:, BLOCK + c : BLOCK + c + 1])
        turned = jnp.where(
            even, -pltpu.roll(w[head], LANES - BLOCK, 1), pltpu.roll(w[head], BLOCK, 1)
        )
        for t in range(STEP):
            r = (base + t) % 8
            at = slice(r, r + 1)
            if t % 2 == 0:
                nxt = slice(r + 1, r + 2)
                first, second = spread(col_re[t][head][at]), spread(col_re[t + 1][head][nxt])
                x_re, x_im = spread(col_re[t + 1][head][at]), spread(col_im[t + 1][head][at])
                inverse = 1.0 / first
                following = first * (1.0 / (first * second - (x_re * x_re + x_im * x_im)))
            else:
                inverse = following
            scale[head] = jnp.where(rows == r, inverse, scale[head])
            m_re = {g: col_re[t][g] * inverse for g in live}
            m_im = {g: col_im[t][g] * inverse for g in live}
            m_re[head] = jnp.where(rows > r, m_re[head], 0.0)
            m_im[head] = jnp.where(rows > r, m_im[head], 0.0)
            below = [g for g in live if g > head or r < 7]
            for u in range(t + 1, STEP):
                e_re, e_im = spread(col_re[u][head][at]), spread(col_im[u][head][at])
                for g in below:
                    col_re[u][g], col_im[u][g] = (
                        col_re[u][g] - (m_re[g] * e_re - m_im[g] * e_im),
                        col_im[u][g] - (m_re[g] * e_im + m_im[g] * e_re),
                    )
            row, row_turned = spread(w[head][at]), spread(turned[at])
            if r < 7:
                turned = turned - (m_re[head] * row_turned - m_im[head] * row)
            for g in below:
                w[g] = w[g] - (m_re[g] * row + m_im[g] * row_turned)
    return jnp.concatenate(w, axis=0) * jnp.sqrt(jnp.concatenate(scale, axis=0))


def split3(x):
    high = x.astype(jnp.bfloat16)
    rest = x - high.astype(jnp.float32)
    mid = rest.astype(jnp.bfloat16)
    low = (rest - mid.astype(jnp.float32)).astype(jnp.bfloat16)
    return high, mid, low


def dot6(left, right):
    high, mid, low = left
    count = high.shape[0]
    first = mm(jnp.concatenate([high, mid, low], axis=0), right[0], NN, None)
    second = mm(jnp.concatenate([high, mid], axis=0), right[1], NN, None)
    third = mm(high, right[2], NN, None)
    small = first[2 * count :] + second[count:] + third
    return first[:count] + (first[count : 2 * count] + second[:count] + small)


def stack_turned(x, half, sign):
    lane = lax.broadcasted_iota(jnp.int32, (x.shape[0], LANES), 1)
    tail = pltpu.roll(x[:, 2 * half :], 64, 1)
    tail = jnp.where((lane < 64) == (sign > 0), -tail, tail)
    out = []
    for whole, end in zip(split3(x), split3(tail)):
        real, imag = whole[:, :half], whole[:, half : 2 * half]
        real, imag = (-imag, real) if sign > 0 else (imag, -real)
        out.append(jnp.concatenate([whole, jnp.concatenate([real, imag, end], axis=1)], axis=0))
    return out


def adapt_kernel(
    place_ref,
    code_ref,
    chunks_ref,
    steer_re_ref,
    steer_im_ref,
    own_ref,
    other_ref,
    sig_re,
    sig_im,
    x_re,
    x_im,
    train,
    mat,
    v_high,
    v_mid,
    v_low,
    s_high,
    s_mid,
    s_low,
):
    chunk_count, _, _, elements = chunks_ref.shape
    _, bin_dev, beams, _ = own_ref.shape
    gate_dev = (chunks_ref.shape[2] - MASK_ROWS) // 2
    gates = chunk_count * gate_dev
    f32, bf16 = jnp.float32, jnp.bfloat16
    for ref in (sig_re, sig_im):
        ref[0:HEAD] = jnp.zeros((HEAD, elements), f32)
        ref[HEAD + gates :] = jnp.zeros((ref.shape[0] - HEAD - gates, elements), f32)
    diagonal = lax.broadcasted_iota(jnp.int32, (gate_dev, LANES), 0) == lax.broadcasted_iota(
        jnp.int32, (gate_dev, LANES), 1
    )
    masks = []
    for c in range(chunk_count):
        chunk = chunks_ref[c, place_ref[0]].astype(f32)
        at = HEAD + c * gate_dev
        sig_re[at : at + gate_dev] = chunk[:gate_dev]
        sig_im[at : at + gate_dev] = chunk[gate_dev : 2 * gate_dev]
        mask_row = chunk[2 * gate_dev : 2 * gate_dev + 1, :LANES]
        masks.append(jnp.sum(jnp.where(diagonal, mask_row, 0.0), axis=1, keepdims=True))

    tap = (
        lax.broadcasted_iota(jnp.int32, (TILE, LANES), 1)
        - lax.broadcasted_iota(jnp.int32, (TILE, LANES), 0)
        - (HEAD - CODE_REACH)
    )
    band_re = jnp.zeros((TILE, LANES), f32)
    band_im = jnp.zeros((TILE, LANES), f32)
    for t in range(2 * CODE_REACH + 1):
        band_re = jnp.where(tap == t, code_ref[0, t], band_re)
        band_im = jnp.where(tap == t, code_ref[1, t], band_im)
    band = jnp.concatenate(
        [
            jnp.concatenate([band_re, -band_im], axis=1),
            jnp.concatenate([band_im, band_re], axis=1),
        ],
        axis=0,
    )
    bands = split3(band)
    for c in range(gates // TILE):
        at = c * TILE
        window = jnp.concatenate(
            [sig_re[at : at + LANES].astype(bf16), sig_im[at : at + LANES].astype(bf16)], axis=0
        )
        high, mid, low = (mm(part, window, NN, None) for part in bands)
        both = (high + (mid + low)).astype(bf16).astype(f32)
        real, imag = both[:TILE], both[TILE:]
        x_re[at : at + TILE] = real
        x_im[at : at + TILE] = imag
        per = TILE // gate_dev
        mask = jnp.concatenate(masks[c * per : (c + 1) * per], axis=0)
        train[at : at + TILE, :elements] = (real * mask).astype(bf16)
        train[at : at + TILE, elements:] = (imag * mask).astype(bf16)

    a, b = train[:, :elements], train[:, elements:]
    left = jnp.concatenate([a, b], axis=0)
    right = jnp.concatenate([jnp.concatenate([a, -b], axis=1), jnp.concatenate([b, a], axis=1)], axis=0)
    gram = mm(left, right, TN, None) * (1.0 / gates)
    corner = lax.broadcasted_iota(jnp.int32, (elements, elements), 0) == lax.broadcasted_iota(
        jnp.int32, (elements, elements), 1
    )
    mat[:, :elements] = gram[:, :elements] + jnp.where(corner, LOADING, 0.0)
    mat[:, elements : 2 * elements] = gram[:, elements:]

    spare = jnp.zeros((64 - 8 - 2 * gate_dev, elements), f32)
    sides = []
    for steer_ref, ref in ((steer_re_ref, x_re), (steer_im_ref, x_im)):
        sides.append(steer_ref[...])
        for slot in (1, 2):
            at = pl.multiple_of(place_ref[slot] * gate_dev, 8)
            sides.append(ref[pl.ds(at, gate_dev)])
        sides.append(spare)
    mat[:, 2 * elements :] = jnp.concatenate(sides, axis=0).T

    lane = lax.broadcasted_iota(jnp.int32, (BLOCK, BLOCK), 1)
    unit = jnp.where(lax.broadcasted_iota(jnp.int32, (BLOCK, BLOCK), 0) == lane, 1.0, 0.0)
    blank = jnp.zeros((BLOCK, BLOCK), f32)
    steps = elements // BLOCK
    start = lambda k: k * BLOCK // LANES * LANES
    pick = lambda ref, rows, lo: jnp.concatenate(
        [ref[rows, lo:elements], ref[rows, elements + lo : 2 * elements], ref[rows, 2 * elements :]],
        axis=1,
    )
    acc = mat[0:BLOCK]
    for k in range(steps):
        at, nxt = k * BLOCK, (k + 1) * BLOCK
        seen = 2 * at
        first, following = start(k), start(k + 1)
        half = elements - first
        here = at - first
        d_re = acc[:, here : here + BLOCK]
        d_im = acc[:, half + here : half + here + BLOCK]
        panel = stack_turned(acc, half, 1)
        if k + 1 < steps:
            later = pick(mat, slice(nxt, nxt + BLOCK), following)
            if k > 0:
                later = later - dot6(
                    [ref[nxt : nxt + BLOCK, :seen] for ref in (s_high, s_mid, s_low)],
                    [pick(ref, slice(0, seen), following) for ref in (v_high, v_mid, v_low)],
                )
        work = jnp.concatenate([unit, blank, d_re, d_im], axis=1)
        work = eliminate(work)
        solved = dot6(split3(work[:, : 2 * BLOCK]), panel)
        mat[at:nxt, 2 * elements :] = solved[:, 2 * half :]
        if k + 1 < steps:
            drop = following - first
            if drop:
                solved = jnp.concatenate(
                    [solved[:, drop:half], solved[:, half + drop : 2 * half], solved[:, 2 * half :]],
                    axis=1,
                )
            half = elements - following
            trail = stack_turned(solved, half, -1)
            stem = jnp.concatenate([solved[:, :half], solved[:, half : 2 * half]], axis=0).T
            stems = split3(stem[nxt - following :])
            acc = later - dot6([part[:BLOCK] for part in stems], trail)
            for ref, part in zip((v_high, v_mid, v_low), trail):
                rows = slice(seen, seen + 2 * BLOCK)
                ref[rows, following:elements] = part[:, :half]
                ref[rows, elements + following : 2 * elements] = part[:, half : 2 * half]
                ref[rows, 2 * elements :] = part[:, 2 * half :]
            for ref, part in zip((s_high, s_mid, s_low), stems):
                ref[nxt:, seen : seen + 2 * BLOCK] = part

    whitened = mat[:, 2 * elements :]
    inner = mm(whitened, whitened, TN)
    top, low = inner[0:8], pltpu.roll(inner[64:72], 64, 1)
    real = top + low
    imag = pltpu.roll(top - low, 64, 1)
    own_lane = lax.broadcasted_iota(jnp.int32, (8, LANES), 1) == lax.broadcasted_iota(
        jnp.int32, (8, LANES), 0
    )
    response = jnp.sum(jnp.where(own_lane, real, 0.0), axis=1, keepdims=True)
    factor = lax.rsqrt(jnp.where(response > 0.0, response, 1.0))
    both = jnp.concatenate([real * factor, imag * factor], axis=0)
    for ref, shift in ((own_ref, 8), (other_ref, 8 + gate_dev)):
        moved = pltpu.roll(both, LANES - shift, 1)
        for part in range(2):
            rows = moved[8 * part : 8 * part + beams, :gate_dev]
            for b in range(bin_dev):
                ref[part, b] = jnp.where(place_ref[0] == b, rows, 0.0)


def adapt(place, code, chunks, steer_re, steer_im, beams):
    count, bin_dev, rows, elements = chunks.shape
    gate_dev = (rows - MASK_ROWS) // 2
    gates = count * gate_dev
    width = 2 * elements + LANES
    out = (2, bin_dev, beams, gate_dev)
    f32, bf16 = jnp.float32, jnp.bfloat16
    return pl.pallas_call(
        adapt_kernel,
        grid_spec=pltpu.PrefetchScalarGridSpec(
            num_scalar_prefetch=1,
            grid=(1,),
            in_specs=[
                pl.BlockSpec(memory_space=pltpu.SMEM),
                pl.BlockSpec(memory_space=pltpu.VMEM),
                pl.BlockSpec(memory_space=pltpu.VMEM),
                pl.BlockSpec(memory_space=pltpu.VMEM),
            ],
            out_specs=[pl.BlockSpec(memory_space=pltpu.VMEM)] * 2,
            scratch_shapes=[
                pltpu.VMEM((gates - TILE + LANES + HEAD, elements), f32),
                pltpu.VMEM((gates - TILE + LANES + HEAD, elements), f32),
                pltpu.VMEM((gates, elements), f32),
                pltpu.VMEM((gates, elements), f32),
                pltpu.VMEM((gates, 2 * elements), bf16),
                pltpu.VMEM((elements, width), f32),
            ]
            + [pltpu.VMEM((2 * elements, width), bf16)] * 3
            + [pltpu.VMEM((elements, 2 * elements), bf16)] * 3,
        ),
        out_shape=[pltpu.VMEM(out, f32)] * 2,
        name="adapt",
    )(place, code, chunks, steer_re, steer_im)


def channel_kernel(
    raw_ref, taps_hbm, table_hbm, out_ref, raw, filtered, taps_ref, table_ref, arrived, small
):
    elem_dev = arrived.shape[0]
    get_taps = pltpu.make_async_copy(taps_hbm, taps_ref, small.at[0])
    get_table = pltpu.make_async_copy(table_hbm, table_ref, small.at[1])
    get_taps.start()
    dests, bin_dev, lanes = out_ref.shape
    rows = lanes // 2
    gate_dev = rows // elem_dev
    per = gate_dev * 8 * TAPS
    copies = [
        pltpu.make_async_copy(
            raw_ref.at[pl.ds(e * per, per)], raw.at[pl.ds(e * per, per)], arrived.at[e]
        )
        for e in range(elem_dev)
    ]
    for copy in copies:
        copy.start()
    get_table.start()
    get_taps.wait()
    pair = lax.broadcasted_iota(jnp.int32, (8, LANES), 0) // 2
    weights = []
    for t in range(TAPS):
        weight = jnp.zeros((8, LANES), jnp.float32)
        for j in range(CHANNELS // LANES):
            piece = taps_ref[t : t + 1, j * LANES : (j + 1) * LANES]
            weight = jnp.where(pair == j, piece, weight)
        weights.append(weight)
    for e, copy in enumerate(copies):
        copy.wait()
        for g in range(gate_dev):
            at = e * per + g * 8 * TAPS
            piece = raw[at : at + 8 * TAPS].astype(jnp.float32)
            total = piece[0:8] * weights[0]
            for t in range(1, TAPS):
                total = total + piece[8 * t : 8 * t + 8] * weights[t]
            to = (g * elem_dev + e) * 8
            filtered[to : to + 8] = total.astype(jnp.bfloat16).astype(jnp.float32)
    get_table.wait()
    sums = []
    for r in range(2):
        rows_r = jnp.concatenate(
            [filtered[pl.ds(2 * j + r, rows, stride=8)] for j in range(CHANNELS // LANES)], axis=1
        ).astype(jnp.bfloat16)
        sums.append(mm(table_ref[...], rows_r, NT, None))
    half = dests * bin_dev
    re = sums[0][:half] + sums[1][half:]
    im = sums[1][:half] - sums[0][half:]
    spectra = jnp.concatenate([re, im], axis=1).astype(jnp.bfloat16)
    for d in range(dests):
        out_ref[d] = spectra[bin_dev * d : bin_dev * (d + 1)]


def channelize(raw_samples, filter_taps, bin_dev, dop_count):
    elem_dev, gate_dev = raw_samples.shape[:2]
    tiles = CHANNELS // LANES
    flat = raw_samples.reshape(elem_dev, gate_dev, 2, TAPS * tiles, LANES)
    flat = jnp.transpose(flat, (0, 1, 3, 2, 4)).reshape(-1, LANES)
    rows = gate_dev * elem_dev
    table = dft_rows(dop_count * bin_dev)
    return pl.pallas_call(
        channel_kernel,
        in_specs=[pl.BlockSpec(memory_space=pl.ANY)] * 3,
        out_specs=pl.BlockSpec(memory_space=pltpu.VMEM),
        out_shape=pltpu.VMEM((dop_count, bin_dev, 2 * rows), jnp.bfloat16),
        scratch_shapes=[
            pltpu.VMEM(flat.shape, jnp.bfloat16),
            pltpu.VMEM((rows * 8, LANES), jnp.float32),
            pltpu.VMEM(filter_taps.shape, jnp.float32),
            pltpu.VMEM(table.shape, jnp.bfloat16),
            pltpu.SemaphoreType.DMA((elem_dev,)),
            pltpu.SemaphoreType.DMA((2,)),
        ],
        name="channelize",
    )(flat, filter_taps, table)


def steering_rows(steer_row, elements):
    element = jnp.arange(elements, dtype=jnp.int32)
    turn = jnp.mod(
        element[None, :] * (2 * steer_row[:, None] - elements), 2 * elements
    ).astype(jnp.float32)
    phases = turn * (math.pi / elements)
    pad = ((0, 8 - steer_row.shape[0]), (0, 0))
    return jnp.pad(jnp.cos(phases), pad), jnp.pad(jnp.sin(phases), pad)


def shards(raw_samples, filter_taps, range_code, train_mask, steer_index):
    elem_dev, gate_dev = raw_samples.shape[:2]
    bin_dev, beams = steer_index.shape
    dop_count, rng_count = lax.axis_size("dop"), lax.axis_size("rng")
    elements = elem_dev * dop_count
    spectra = channelize(raw_samples, filter_taps, bin_dev, dop_count)
    turned = lax.all_to_all(spectra, "dop", split_axis=0, concat_axis=0, tiled=True)
    turned = turned.reshape(dop_count, bin_dev, 2 * gate_dev, elem_dev)
    turned = jnp.transpose(turned, (1, 2, 0, 3)).reshape(bin_dev, 2 * gate_dev, elements)
    mask = jnp.pad(
        train_mask.astype(jnp.bfloat16)[:, None, :],
        ((0, 0), (0, MASK_ROWS - 1), (0, elements - gate_dev)),
    )
    chunk = jnp.concatenate([turned, mask], axis=1)
    chunks = lax.all_gather(chunk, "rng", axis=0, tiled=False)
    position = lax.axis_index("rng")
    core = position % bin_dev
    place = jnp.stack([core, position, position ^ 1]).astype(jnp.int32)
    steer_row = lax.dynamic_index_in_dim(steer_index, core, 0, keepdims=False)
    steer_re, steer_im = steering_rows(steer_row, elements)
    chunks, steer_re, steer_im = (
        pltpu.with_memory_space_constraint(x, pltpu.VMEM) for x in (chunks, steer_re, steer_im)
    )
    own, other = adapt(place, range_code, chunks, steer_re, steer_im, beams)
    swapped = lax.ppermute(other, "rng", [(i, i ^ 1) for i in range(rng_count)])
    return own + swapped


def solution(mesh):
    return jax.shard_map(
        shards,
        mesh=mesh,
        in_specs=(P("dop", "rng", None, None), P(), P(), P("dop", "rng"), P("dop", None)),
        out_specs=P(None, "dop", None, "rng"),
        check_vma=False,
    )
```

```python
import math

import jax
import jax.numpy as jnp
import numpy as np
from jax import lax
from jax.experimental import pallas as pl
from jax.experimental.pallas import tpu as pltpu
from jax.sharding import PartitionSpec as P

CHANNELS = 512
TAPS = 8
CODE_REACH = 3
LOADING = 0.25
BLOCK = 32
STEP = 8
LANES = 128
HEAD = 8
TILE = 96
MASK_ROWS = 8

HIGHEST = lax.Precision.HIGHEST


def dft_rows(bin_total):
    mode = np.arange(CHANNELS, dtype=np.int64)[None, :]
    turn = (mode * np.arange(bin_total, dtype=np.int64)[:, None]) % CHANNELS
    phases = turn.astype(np.float32) * np.float32(2.0 * math.pi / CHANNELS)
    scale = np.float32(math.sqrt(CHANNELS))
    both = np.concatenate([np.cos(phases) / scale, np.sin(phases) / scale], axis=0)
    return jnp.asarray(both, jnp.bfloat16)


def mm(a, b, dims, precision=HIGHEST):
    return lax.dot_general(
        a, b, (dims, ((), ())), precision=precision, preferred_element_type=jnp.float32
    )


NN = ((1,), (0,))
TN = ((0,), (0,))
NT = ((1,), (1,))


def eliminate(work):
    count = BLOCK // 8
    w = [work[8 * g : 8 * g + 8] for g in range(count)]
    rows = lax.broadcasted_iota(jnp.int32, (8, LANES), 0)
    even = lax.broadcasted_iota(jnp.int32, (8, LANES), 1) // BLOCK % 2 == 0
    scale = [jnp.zeros((8, LANES), jnp.float32)] * count
    spread = lambda x: jnp.broadcast_to(x, (8, LANES))
    for base in range(0, BLOCK, STEP):
        head = base // 8
        live = range(head, count)
        col_re = [{} for _ in range(STEP)]
        col_im = [{} for _ in range(STEP)]
        for g in live:
            for t in range(STEP):
                c = 2 * BLOCK + base + t
                col_re[t][g] = spread(w[g][:, c : c + 1])
                col_im[t][g] = spread(w[g][:, BLOCK + c : BLOCK + c + 1])
        turned = jnp.where(
            even, -pltpu.roll(w[head], LANES - BLOCK, 1), pltpu.roll(w[head], BLOCK, 1)
        )
        for t in range(STEP):
            r = (base + t) % 8
            at = slice(r, r + 1)
            if t % 2 == 0:
                nxt = slice(r + 1, r + 2)
                first, second = spread(col_re[t][head][at]), spread(col_re[t + 1][head][nxt])
                x_re, x_im = spread(col_re[t + 1][head][at]), spread(col_im[t + 1][head][at])
                inverse = 1.0 / first
                following = first * (1.0 / (first * second - (x_re * x_re + x_im * x_im)))
            else:
                inverse = following
            scale[head] = jnp.where(rows == r, inverse, scale[head])
            m_re = {g: col_re[t][g] * inverse for g in live}
            m_im = {g: col_im[t][g] * inverse for g in live}
            m_re[head] = jnp.where(rows > r, m_re[head], 0.0)
            m_im[head] = jnp.where(rows > r, m_im[head], 0.0)
            below = [g for g in live if g > head or r < 7]
            for u in range(t + 1, STEP):
                e_re, e_im = spread(col_re[u][head][at]), spread(col_im[u][head][at])
                for g in below:
                    col_re[u][g], col_im[u][g] = (
                        col_re[u][g] - (m_re[g] * e_re - m_im[g] * e_im),
                        col_im[u][g] - (m_re[g] * e_im + m_im[g] * e_re),
                    )
            row, row_turned = spread(w[head][at]), spread(turned[at])
            if r < 7:
                turned = turned - (m_re[head] * row_turned - m_im[head] * row)
            for g in below:
                w[g] = w[g] - (m_re[g] * row + m_im[g] * row_turned)
    return jnp.concatenate(w, axis=0) * jnp.sqrt(jnp.concatenate(scale, axis=0))


def split3(x):
    high = x.astype(jnp.bfloat16)
    rest = x - high.astype(jnp.float32)
    mid = rest.astype(jnp.bfloat16)
    low = (rest - mid.astype(jnp.float32)).astype(jnp.bfloat16)
    return high, mid, low


def dot6(left, right):
    high, mid, low = left
    count = high.shape[0]
    first = mm(jnp.concatenate([high, mid, low], axis=0), right[0], NN, None)
    second = mm(jnp.concatenate([high, mid], axis=0), right[1], NN, None)
    third = mm(high, right[2], NN, None)
    small = first[2 * count :] + second[count:] + third
    return first[:count] + (first[count : 2 * count] + second[:count] + small)


def stack_turned(x, half, sign):
    lane = lax.broadcasted_iota(jnp.int32, (x.shape[0], LANES), 1)
    tail = pltpu.roll(x[:, 2 * half :], 64, 1)
    tail = jnp.where((lane < 64) == (sign > 0), -tail, tail)
    out = []
    for whole, end in zip(split3(x), split3(tail)):
        real, imag = whole[:, :half], whole[:, half : 2 * half]
        real, imag = (-imag, real) if sign > 0 else (imag, -real)
        out.append(jnp.concatenate([whole, jnp.concatenate([real, imag, end], axis=1)], axis=0))
    return out


def adapt_kernel(
    code_ref,
    chunks_ref,
    steer_re_ref,
    steer_im_ref,
    own_ref,
    other_ref,
    sig_re,
    sig_im,
    x_re,
    x_im,
    train,
    mat,
    v_high,
    v_mid,
    v_low,
    s_high,
    s_mid,
    s_low,
):
    chunk_count, _, _, elements = chunks_ref.shape
    _, bin_dev, beams, _ = own_ref.shape
    position = lax.axis_index("rng")
    core = position & (bin_dev - 1)
    gate_dev = (chunks_ref.shape[2] - MASK_ROWS) // 2
    gates = chunk_count * gate_dev
    f32, bf16 = jnp.float32, jnp.bfloat16
    for ref in (sig_re, sig_im):
        ref[0:HEAD] = jnp.zeros((HEAD, elements), f32)
        ref[HEAD + gates :] = jnp.zeros((ref.shape[0] - HEAD - gates, elements), f32)
    diagonal = lax.broadcasted_iota(jnp.int32, (gate_dev, LANES), 0) == lax.broadcasted_iota(
        jnp.int32, (gate_dev, LANES), 1
    )
    masks = []
    for c in range(chunk_count):
        chunk = chunks_ref[c, core].astype(f32)
        at = HEAD + c * gate_dev
        sig_re[at : at + gate_dev] = chunk[:gate_dev]
        sig_im[at : at + gate_dev] = chunk[gate_dev : 2 * gate_dev]
        mask_row = chunk[2 * gate_dev : 2 * gate_dev + 1, :LANES]
        masks.append(jnp.sum(jnp.where(diagonal, mask_row, 0.0), axis=1, keepdims=True))

    tap = (
        lax.broadcasted_iota(jnp.int32, (TILE, LANES), 1)
        - lax.broadcasted_iota(jnp.int32, (TILE, LANES), 0)
        - (HEAD - CODE_REACH)
    )
    band_re = jnp.zeros((TILE, LANES), f32)
    band_im = jnp.zeros((TILE, LANES), f32)
    for t in range(2 * CODE_REACH + 1):
        band_re = jnp.where(tap == t, code_ref[0:1, t : t + 1], band_re)
        band_im = jnp.where(tap == t, code_ref[1:2, t : t + 1], band_im)
    band = jnp.concatenate(
        [
            jnp.concatenate([band_re, -band_im], axis=1),
            jnp.concatenate([band_im, band_re], axis=1),
        ],
        axis=0,
    )
    bands = split3(band)
    for c in range(gates // TILE):
        at = c * TILE
        window = jnp.concatenate(
            [sig_re[at : at + LANES].astype(bf16), sig_im[at : at + LANES].astype(bf16)], axis=0
        )
        high, mid, low = (mm(part, window, NN, None) for part in bands)
        both = (high + (mid + low)).astype(bf16).astype(f32)
        real, imag = both[:TILE], both[TILE:]
        x_re[at : at + TILE] = real
        x_im[at : at + TILE] = imag
        per = TILE // gate_dev
        mask = jnp.concatenate(masks[c * per : (c + 1) * per], axis=0)
        train[at : at + TILE, :elements] = (real * mask).astype(bf16)
        train[at : at + TILE, elements:] = (imag * mask).astype(bf16)

    a, b = train[:, :elements], train[:, elements:]
    left = jnp.concatenate([a, b], axis=0)
    right = jnp.concatenate([jnp.concatenate([a, -b], axis=1), jnp.concatenate([b, a], axis=1)], axis=0)
    gram = mm(left, right, TN, None) * (1.0 / gates)
    corner = lax.broadcasted_iota(jnp.int32, (elements, elements), 0) == lax.broadcasted_iota(
        jnp.int32, (elements, elements), 1
    )
    mat[:, :elements] = gram[:, :elements] + jnp.where(corner, LOADING, 0.0)
    mat[:, elements : 2 * elements] = gram[:, elements:]

    spare = jnp.zeros((64 - 8 - 2 * gate_dev, elements), f32)
    sides = []
    for steer_ref, ref in ((steer_re_ref, x_re), (steer_im_ref, x_im)):
        sides.append(steer_ref[...])
        for place in (position, position ^ 1):
            at = pl.multiple_of(place * gate_dev, 8)
            sides.append(ref[pl.ds(at, gate_dev)])
        sides.append(spare)
    mat[:, 2 * elements :] = jnp.concatenate(sides, axis=0).T

    lane = lax.broadcasted_iota(jnp.int32, (BLOCK, BLOCK), 1)
    unit = jnp.where(lax.broadcasted_iota(jnp.int32, (BLOCK, BLOCK), 0) == lane, 1.0, 0.0)
    blank = jnp.zeros((BLOCK, BLOCK), f32)
    steps = elements // BLOCK
    start = lambda k: k * BLOCK // LANES * LANES
    pick = lambda ref, rows, lo: jnp.concatenate(
        [ref[rows, lo:elements], ref[rows, elements + lo : 2 * elements], ref[rows, 2 * elements :]],
        axis=1,
    )
    acc = mat[0:BLOCK]
    for k in range(steps):
        at, nxt = k * BLOCK, (k + 1) * BLOCK
        seen = 2 * at
        first, following = start(k), start(k + 1)
        half = elements - first
        here = at - first
        d_re = acc[:, here : here + BLOCK]
        d_im = acc[:, half + here : half + here + BLOCK]
        panel = stack_turned(acc, half, 1)
        if k + 1 < steps:
            later = pick(mat, slice(nxt, nxt + BLOCK), following)
            if k > 0:
                later = later - dot6(
                    [ref[nxt : nxt + BLOCK, :seen] for ref in (s_high, s_mid, s_low)],
                    [pick(ref, slice(0, seen), following) for ref in (v_high, v_mid, v_low)],
                )
        work = jnp.concatenate([unit, blank, d_re, d_im], axis=1)
        work = eliminate(work)
        solved = dot6(split3(work[:, : 2 * BLOCK]), panel)
        mat[at:nxt, 2 * elements :] = solved[:, 2 * half :]
        if k + 1 < steps:
            drop = following - first
            if drop:
                solved = jnp.concatenate(
                    [solved[:, drop:half], solved[:, half + drop : 2 * half], solved[:, 2 * half :]],
                    axis=1,
                )
            half = elements - following
            trail = stack_turned(solved, half, -1)
            stem = jnp.concatenate([solved[:, :half], solved[:, half : 2 * half]], axis=0).T
            stems = split3(stem[nxt - following :])
            acc = later - dot6([part[:BLOCK] for part in stems], trail)
            for ref, part in zip((v_high, v_mid, v_low), trail):
                rows = slice(seen, seen + 2 * BLOCK)
                ref[rows, following:elements] = part[:, :half]
                ref[rows, elements + following : 2 * elements] = part[:, half : 2 * half]
                ref[rows, 2 * elements :] = part[:, 2 * half :]
            for ref, part in zip((s_high, s_mid, s_low), stems):
                ref[nxt:, seen : seen + 2 * BLOCK] = part

    whitened = mat[:, 2 * elements :]
    upright = whitened.T
    beams_only = jnp.concatenate([upright[0:8], upright[64:72]], axis=0)
    inner = dot6(split3(beams_only), split3(whitened))
    top, low = inner[0:8], pltpu.roll(inner[8:16], 64, 1)
    real = top + low
    imag = pltpu.roll(top - low, 64, 1)
    own_lane = lax.broadcasted_iota(jnp.int32, (8, LANES), 1) == lax.broadcasted_iota(
        jnp.int32, (8, LANES), 0
    )
    response = jnp.sum(jnp.where(own_lane, real, 0.0), axis=1, keepdims=True)
    factor = lax.rsqrt(jnp.where(response > 0.0, response, 1.0))
    both = jnp.concatenate([real * factor, imag * factor], axis=0)
    for ref, shift in ((own_ref, 8), (other_ref, 8 + gate_dev)):
        moved = pltpu.roll(both, LANES - shift, 1)
        for part in range(2):
            rows = moved[8 * part : 8 * part + beams, :gate_dev]
            for b in range(bin_dev):
                ref[part, b] = jnp.where(core == b, rows, 0.0)


def adapt(code, chunks, steer_re, steer_im, beams):
    count, bin_dev, rows, elements = chunks.shape
    gate_dev = (rows - MASK_ROWS) // 2
    gates = count * gate_dev
    width = 2 * elements + LANES
    out = (2, bin_dev, beams, gate_dev)
    f32, bf16 = jnp.float32, jnp.bfloat16
    on_chip = [
        pltpu.with_memory_space_constraint(x, pltpu.VMEM)
        for x in (code, chunks, steer_re, steer_im)
    ]
    return pl.pallas_call(
        adapt_kernel,
        in_specs=[pl.BlockSpec(memory_space=pltpu.VMEM)] * 4,
        out_specs=[pl.BlockSpec(memory_space=pltpu.VMEM)] * 2,
        out_shape=[pltpu.VMEM(out, f32)] * 2,
        scratch_shapes=[
            pltpu.VMEM((gates - TILE + LANES + HEAD, elements), f32),
            pltpu.VMEM((gates - TILE + LANES + HEAD, elements), f32),
            pltpu.VMEM((gates, elements), f32),
            pltpu.VMEM((gates, elements), f32),
            pltpu.VMEM((gates, 2 * elements), bf16),
            pltpu.VMEM((elements, width), f32),
        ]
        + [pltpu.VMEM((2 * elements, width), bf16)] * 3
        + [pltpu.VMEM((elements, 2 * elements), bf16)] * 3,
        name="adapt",
    )(*on_chip)


def channel_kernel(
    raw_ref, taps_hbm, table_hbm, out_ref, raw, filtered, taps_ref, table_ref, arrived, small
):
    elem_dev = arrived.shape[0]
    get_taps = pltpu.make_async_copy(taps_hbm, taps_ref, small.at[0])
    get_table = pltpu.make_async_copy(table_hbm, table_ref, small.at[1])
    get_taps.start()
    dests, bin_dev, lanes = out_ref.shape
    rows = lanes // 2
    gate_dev = rows // elem_dev
    per = gate_dev * 8 * TAPS
    copies = [
        pltpu.make_async_copy(
            raw_ref.at[pl.ds(e * per, per)], raw.at[pl.ds(e * per, per)], arrived.at[e]
        )
        for e in range(elem_dev)
    ]
    for copy in copies:
        copy.start()
    get_table.start()
    get_taps.wait()
    pair = lax.broadcasted_iota(jnp.int32, (8, LANES), 0) // 2
    weights = []
    for t in range(TAPS):
        weight = jnp.zeros((8, LANES), jnp.float32)
        for j in range(CHANNELS // LANES):
            piece = taps_ref[t : t + 1, j * LANES : (j + 1) * LANES]
            weight = jnp.where(pair == j, piece, weight)
        weights.append(weight)
    for e, copy in enumerate(copies):
        copy.wait()
        for g in range(gate_dev):
            at = e * per + g * 8 * TAPS
            piece = raw[at : at + 8 * TAPS].astype(jnp.float32)
            total = piece[0:8] * weights[0]
            for t in range(1, TAPS):
                total = total + piece[8 * t : 8 * t + 8] * weights[t]
            to = (g * elem_dev + e) * 8
            filtered[to : to + 8] = total.astype(jnp.bfloat16).astype(jnp.float32)
    get_table.wait()
    sums = []
    for r in range(2):
        rows_r = jnp.concatenate(
            [filtered[pl.ds(2 * j + r, rows, stride=8)] for j in range(CHANNELS // LANES)], axis=1
        ).astype(jnp.bfloat16)
        sums.append(mm(table_ref[...], rows_r, NT, None))
    half = dests * bin_dev
    re = sums[0][:half] + sums[1][half:]
    im = sums[1][:half] - sums[0][half:]
    spectra = jnp.concatenate([re, im], axis=1).astype(jnp.bfloat16)
    for d in range(dests):
        out_ref[d] = spectra[bin_dev * d : bin_dev * (d + 1)]


def channelize(raw_samples, filter_taps, bin_dev, dop_count):
    elem_dev, gate_dev = raw_samples.shape[:2]
    tiles = CHANNELS // LANES
    flat = raw_samples.reshape(elem_dev, gate_dev, 2, TAPS * tiles, LANES)
    flat = jnp.transpose(flat, (0, 1, 3, 2, 4)).reshape(-1, LANES)
    rows = gate_dev * elem_dev
    table = dft_rows(dop_count * bin_dev)
    return pl.pallas_call(
        channel_kernel,
        in_specs=[pl.BlockSpec(memory_space=pl.ANY)] * 3,
        out_specs=pl.BlockSpec(memory_space=pltpu.VMEM),
        out_shape=pltpu.VMEM((dop_count, bin_dev, 2 * rows), jnp.bfloat16),
        scratch_shapes=[
            pltpu.VMEM(flat.shape, jnp.bfloat16),
            pltpu.VMEM((rows * 8, LANES), jnp.float32),
            pltpu.VMEM(filter_taps.shape, jnp.float32),
            pltpu.VMEM(table.shape, jnp.bfloat16),
            pltpu.SemaphoreType.DMA((elem_dev,)),
            pltpu.SemaphoreType.DMA((2,)),
        ],
        name="channelize",
    )(flat, filter_taps, table)


def steering_rows(steer_row, elements):
    element = jnp.arange(elements, dtype=jnp.int32)
    turn = jnp.mod(
        element[None, :] * (2 * steer_row[:, None] - elements), 2 * elements
    ).astype(jnp.float32)
    phases = turn * (math.pi / elements)
    pad = ((0, 8 - steer_row.shape[0]), (0, 0))
    return jnp.pad(jnp.cos(phases), pad), jnp.pad(jnp.sin(phases), pad)


def shards(raw_samples, filter_taps, range_code, train_mask, steer_index):
    elem_dev, gate_dev = raw_samples.shape[:2]
    bin_dev, beams = steer_index.shape
    dop_count, rng_count = lax.axis_size("dop"), lax.axis_size("rng")
    elements = elem_dev * dop_count
    spectra = channelize(raw_samples, filter_taps, bin_dev, dop_count)
    turned = lax.all_to_all(spectra, "dop", split_axis=0, concat_axis=0, tiled=True)
    turned = turned.reshape(dop_count, bin_dev, 2 * gate_dev, elem_dev)
    turned = jnp.transpose(turned, (1, 2, 0, 3)).reshape(bin_dev, 2 * gate_dev, elements)
    mask = jnp.pad(
        train_mask.astype(jnp.bfloat16)[:, None, :],
        ((0, 0), (0, MASK_ROWS - 1), (0, elements - gate_dev)),
    )
    chunk = jnp.concatenate([turned, mask], axis=1)
    chunks = lax.all_gather(chunk, "rng", axis=0, tiled=False)
    core = lax.axis_index("rng") % bin_dev
    steer_row = lax.dynamic_index_in_dim(steer_index, core, 0, keepdims=False)
    steer_re, steer_im = steering_rows(steer_row, elements)
    own, other = adapt(range_code, chunks, steer_re, steer_im, beams)
    swapped = lax.ppermute(other, "rng", [(i, i ^ 1) for i in range(rng_count)])
    return own + swapped


def solution(mesh):
    return jax.shard_map(
        shards,
        mesh=mesh,
        in_specs=(P("dop", "rng", None, None), P(), P(), P("dop", "rng"), P("dop", None)),
        out_specs=P(None, "dop", None, "rng"),
        check_vma=False,
    )
```

```python
import math

import jax
import jax.numpy as jnp
import numpy as np
from jax import lax
from jax.experimental import pallas as pl
from jax.experimental.pallas import tpu as pltpu
from jax.sharding import PartitionSpec as P

CHANNELS = 512
TAPS = 8
CODE_REACH = 3
LOADING = 0.25
BLOCK = 32
STEP = 8
LANES = 128
HEAD = 8
TILE = 96
MASK_ROWS = 8

HIGHEST = lax.Precision.HIGHEST


def dft_rows(bin_total):
    mode = np.arange(CHANNELS, dtype=np.int64)[None, :]
    turn = (mode * np.arange(bin_total, dtype=np.int64)[:, None]) % CHANNELS
    phases = turn.astype(np.float32) * np.float32(2.0 * math.pi / CHANNELS)
    scale = np.float32(math.sqrt(CHANNELS))
    both = np.concatenate([np.cos(phases) / scale, np.sin(phases) / scale], axis=0)
    return jnp.asarray(both, jnp.bfloat16)


def mm(a, b, dims, precision=HIGHEST):
    return lax.dot_general(
        a, b, (dims, ((), ())), precision=precision, preferred_element_type=jnp.float32
    )


NN = ((1,), (0,))
TN = ((0,), (0,))
NT = ((1,), (1,))


def eliminate(work):
    count = BLOCK // 8
    w = [work[8 * g : 8 * g + 8] for g in range(count)]
    rows = lax.broadcasted_iota(jnp.int32, (8, LANES), 0)
    even = lax.broadcasted_iota(jnp.int32, (8, LANES), 1) // BLOCK % 2 == 0
    scale = [jnp.zeros((8, LANES), jnp.float32)] * count
    spread = lambda x: jnp.broadcast_to(x, (8, LANES))
    for base in range(0, BLOCK, STEP):
        head = base // 8
        live = range(head, count)
        col_re = [{} for _ in range(STEP)]
        col_im = [{} for _ in range(STEP)]
        for g in live:
            for t in range(STEP):
                c = 2 * BLOCK + base + t
                col_re[t][g] = spread(w[g][:, c : c + 1])
                col_im[t][g] = spread(w[g][:, BLOCK + c : BLOCK + c + 1])
        turned = jnp.where(
            even, -pltpu.roll(w[head], LANES - BLOCK, 1), pltpu.roll(w[head], BLOCK, 1)
        )
        for t in range(STEP):
            r = (base + t) % 8
            at = slice(r, r + 1)
            if t % 2 == 0:
                nxt = slice(r + 1, r + 2)
                first, second = spread(col_re[t][head][at]), spread(col_re[t + 1][head][nxt])
                x_re, x_im = spread(col_re[t + 1][head][at]), spread(col_im[t + 1][head][at])
                inverse = 1.0 / first
                following = first * (1.0 / (first * second - (x_re * x_re + x_im * x_im)))
            else:
                inverse = following
            scale[head] = jnp.where(rows == r, inverse, scale[head])
            m_re = {g: col_re[t][g] * inverse for g in live}
            m_im = {g: col_im[t][g] * inverse for g in live}
            m_re[head] = jnp.where(rows > r, m_re[head], 0.0)
            m_im[head] = jnp.where(rows > r, m_im[head], 0.0)
            below = [g for g in live if g > head or r < 7]
            for u in range(t + 1, STEP):
                e_re, e_im = spread(col_re[u][head][at]), spread(col_im[u][head][at])
                for g in below:
                    col_re[u][g], col_im[u][g] = (
                        col_re[u][g] - (m_re[g] * e_re - m_im[g] * e_im),
                        col_im[u][g] - (m_re[g] * e_im + m_im[g] * e_re),
                    )
            row, row_turned = spread(w[head][at]), spread(turned[at])
            if r < 7:
                turned = turned - (m_re[head] * row_turned - m_im[head] * row)
            for g in below:
                w[g] = w[g] - (m_re[g] * row + m_im[g] * row_turned)
    return jnp.concatenate(w, axis=0) * jnp.sqrt(jnp.concatenate(scale, axis=0))


def split3(x):
    high = x.astype(jnp.bfloat16)
    rest = x - high.astype(jnp.float32)
    mid = rest.astype(jnp.bfloat16)
    low = (rest - mid.astype(jnp.float32)).astype(jnp.bfloat16)
    return high, mid, low


def dot6(left, right):
    high, mid, low = left
    count = high.shape[0]
    first = mm(jnp.concatenate([high, mid, low], axis=0), right[0], NN, None)
    second = mm(jnp.concatenate([high, mid], axis=0), right[1], NN, None)
    third = mm(high, right[2], NN, None)
    small = first[2 * count :] + second[count:] + third
    return first[:count] + (first[count : 2 * count] + second[:count] + small)


def stack_turned(x, half, sign):
    lane = lax.broadcasted_iota(jnp.int32, (x.shape[0], LANES), 1)
    tail = pltpu.roll(x[:, 2 * half :], 64, 1)
    tail = jnp.where((lane < 64) == (sign > 0), -tail, tail)
    out = []
    for whole, end in zip(split3(x), split3(tail)):
        real, imag = whole[:, :half], whole[:, half : 2 * half]
        real, imag = (-imag, real) if sign > 0 else (imag, -real)
        out.append(jnp.concatenate([whole, jnp.concatenate([real, imag, end], axis=1)], axis=0))
    return out


def adapt_kernel(
    code_ref,
    chunks_ref,
    steer_re_ref,
    steer_im_ref,
    own_ref,
    other_ref,
    sig_re,
    sig_im,
    x_re,
    x_im,
    train,
    mat,
    v_high,
    v_mid,
    v_low,
    s_high,
    s_mid,
    s_low,
):
    chunk_count, tiles, _, elements = chunks_ref.shape
    _, bin_dev, beams, gate_dev = own_ref.shape
    per_bin = (tiles - 1) // bin_dev
    position = lax.axis_index("rng")
    core = position & (bin_dev - 1)
    gates = chunk_count * gate_dev
    f32, bf16 = jnp.float32, jnp.bfloat16
    for ref in (sig_re, sig_im):
        ref[0:HEAD] = jnp.zeros((HEAD, elements), f32)
        ref[HEAD + gates :] = jnp.zeros((ref.shape[0] - HEAD - gates, elements), f32)
    diagonal = lax.broadcasted_iota(jnp.int32, (gate_dev, LANES), 0) == lax.broadcasted_iota(
        jnp.int32, (gate_dev, LANES), 1
    )
    masks = []
    for c in range(chunk_count):
        chunk = chunks_ref[c, pl.ds(core * per_bin, per_bin)].astype(f32)
        chunk = chunk.reshape(2 * gate_dev, elements)
        at = HEAD + c * gate_dev
        sig_re[at : at + gate_dev] = chunk[:gate_dev]
        sig_im[at : at + gate_dev] = chunk[gate_dev : 2 * gate_dev]
        rows = chunks_ref[c, tiles - 1, :, :LANES].astype(f32)
        mask_row = jnp.where(core == 0, rows[0:1], rows[1:2])
        masks.append(jnp.sum(jnp.where(diagonal, mask_row, 0.0), axis=1, keepdims=True))

    tap = (
        lax.broadcasted_iota(jnp.int32, (TILE, LANES), 1)
        - lax.broadcasted_iota(jnp.int32, (TILE, LANES), 0)
        - (HEAD - CODE_REACH)
    )
    band_re = jnp.zeros((TILE, LANES), f32)
    band_im = jnp.zeros((TILE, LANES), f32)
    for t in range(2 * CODE_REACH + 1):
        band_re = jnp.where(tap == t, code_ref[0:1, t : t + 1], band_re)
        band_im = jnp.where(tap == t, code_ref[1:2, t : t + 1], band_im)
    band = jnp.concatenate(
        [
            jnp.concatenate([band_re, -band_im], axis=1),
            jnp.concatenate([band_im, band_re], axis=1),
        ],
        axis=0,
    )
    bands = split3(band)
    for c in range(gates // TILE):
        at = c * TILE
        window = jnp.concatenate(
            [sig_re[at : at + LANES].astype(bf16), sig_im[at : at + LANES].astype(bf16)], axis=0
        )
        high, mid, low = (mm(part, window, NN, None) for part in bands)
        both = (high + (mid + low)).astype(bf16).astype(f32)
        real, imag = both[:TILE], both[TILE:]
        x_re[at : at + TILE] = real
        x_im[at : at + TILE] = imag
        per = TILE // gate_dev
        mask = jnp.concatenate(masks[c * per : (c + 1) * per], axis=0)
        train[at : at + TILE, :elements] = (real * mask).astype(bf16)
        train[at : at + TILE, elements:] = (imag * mask).astype(bf16)

    a, b = train[:, :elements], train[:, elements:]
    left = jnp.concatenate([a, b], axis=0)
    right = jnp.concatenate([jnp.concatenate([a, -b], axis=1), jnp.concatenate([b, a], axis=1)], axis=0)
    gram = mm(left, right, TN, None) * (1.0 / gates)
    corner = lax.broadcasted_iota(jnp.int32, (elements, elements), 0) == lax.broadcasted_iota(
        jnp.int32, (elements, elements), 1
    )
    mat[:, :elements] = gram[:, :elements] + jnp.where(corner, LOADING, 0.0)
    mat[:, elements : 2 * elements] = gram[:, elements:]

    spare = jnp.zeros((64 - 8 - 2 * gate_dev, elements), f32)
    sides = []
    for steer_ref, ref in ((steer_re_ref, x_re), (steer_im_ref, x_im)):
        sides.append(steer_ref[...])
        for place in (position, position ^ 1):
            at = pl.multiple_of(place * gate_dev, 8)
            sides.append(ref[pl.ds(at, gate_dev)])
        sides.append(spare)
    mat[:, 2 * elements :] = jnp.concatenate(sides, axis=0).T

    lane = lax.broadcasted_iota(jnp.int32, (BLOCK, BLOCK), 1)
    unit = jnp.where(lax.broadcasted_iota(jnp.int32, (BLOCK, BLOCK), 0) == lane, 1.0, 0.0)
    blank = jnp.zeros((BLOCK, BLOCK), f32)
    steps = elements // BLOCK
    start = lambda k: k * BLOCK // LANES * LANES
    pick = lambda ref, rows, lo: jnp.concatenate(
        [ref[rows, lo:elements], ref[rows, elements + lo : 2 * elements], ref[rows, 2 * elements :]],
        axis=1,
    )
    acc = mat[0:BLOCK]
    for k in range(steps):
        at, nxt = k * BLOCK, (k + 1) * BLOCK
        seen = 2 * at
        first, following = start(k), start(k + 1)
        half = elements - first
        here = at - first
        d_re = acc[:, here : here + BLOCK]
        d_im = acc[:, half + here : half + here + BLOCK]
        panel = stack_turned(acc, half, 1)
        if k + 1 < steps:
            later = pick(mat, slice(nxt, nxt + BLOCK), following)
            if k > 0:
                later = later - dot6(
                    [ref[nxt : nxt + BLOCK, :seen] for ref in (s_high, s_mid, s_low)],
                    [pick(ref, slice(0, seen), following) for ref in (v_high, v_mid, v_low)],
                )
        work = jnp.concatenate([unit, blank, d_re, d_im], axis=1)
        work = eliminate(work)
        solved = dot6(split3(work[:, : 2 * BLOCK]), panel)
        mat[at:nxt, 2 * elements :] = solved[:, 2 * half :]
        if k + 1 < steps:
            drop = following - first
            if drop:
                solved = jnp.concatenate(
                    [solved[:, drop:half], solved[:, half + drop : 2 * half], solved[:, 2 * half :]],
                    axis=1,
                )
            half = elements - following
            trail = stack_turned(solved, half, -1)
            stem = jnp.concatenate([solved[:, :half], solved[:, half : 2 * half]], axis=0).T
            stems = split3(stem[nxt - following :])
            acc = later - dot6([part[:BLOCK] for part in stems], trail)
            for ref, part in zip((v_high, v_mid, v_low), trail):
                rows = slice(seen, seen + 2 * BLOCK)
                ref[rows, following:elements] = part[:, :half]
                ref[rows, elements + following : 2 * elements] = part[:, half : 2 * half]
                ref[rows, 2 * elements :] = part[:, 2 * half :]
            for ref, part in zip((s_high, s_mid, s_low), stems):
                ref[nxt:, seen : seen + 2 * BLOCK] = part

    whitened = mat[:, 2 * elements :]
    upright = whitened.T
    beams_only = jnp.concatenate([upright[0:8], upright[64:72]], axis=0)
    inner = dot6(split3(beams_only), split3(whitened))
    top, low = inner[0:8], pltpu.roll(inner[8:16], 64, 1)
    real = top + low
    imag = pltpu.roll(top - low, 64, 1)
    own_lane = lax.broadcasted_iota(jnp.int32, (8, LANES), 1) == lax.broadcasted_iota(
        jnp.int32, (8, LANES), 0
    )
    response = jnp.sum(jnp.where(own_lane, real, 0.0), axis=1, keepdims=True)
    factor = lax.rsqrt(jnp.where(response > 0.0, response, 1.0))
    both = jnp.concatenate([real * factor, imag * factor], axis=0)
    for ref, shift in ((own_ref, 8), (other_ref, 8 + gate_dev)):
        moved = pltpu.roll(both, LANES - shift, 1)
        for part in range(2):
            rows = moved[8 * part : 8 * part + beams, :gate_dev]
            for b in range(bin_dev):
                ref[part, b] = jnp.where(core == b, rows, 0.0)


def adapt(code, chunks, steer_re, steer_im, bin_dev, beams):
    count, tiles, _, elements = chunks.shape
    gate_dev = (tiles - 1) * MASK_ROWS // (2 * bin_dev)
    gates = count * gate_dev
    width = 2 * elements + LANES
    out = (2, bin_dev, beams, gate_dev)
    f32, bf16 = jnp.float32, jnp.bfloat16
    on_chip = [
        pltpu.with_memory_space_constraint(x, pltpu.VMEM)
        for x in (code, chunks, steer_re, steer_im)
    ]
    return pl.pallas_call(
        adapt_kernel,
        in_specs=[pl.BlockSpec(memory_space=pltpu.VMEM)] * 4,
        out_specs=[pl.BlockSpec(memory_space=pltpu.VMEM)] * 2,
        out_shape=[pltpu.VMEM(out, f32)] * 2,
        scratch_shapes=[
            pltpu.VMEM((gates - TILE + LANES + HEAD, elements), f32),
            pltpu.VMEM((gates - TILE + LANES + HEAD, elements), f32),
            pltpu.VMEM((gates, elements), f32),
            pltpu.VMEM((gates, elements), f32),
            pltpu.VMEM((gates, 2 * elements), bf16),
            pltpu.VMEM((elements, width), f32),
        ]
        + [pltpu.VMEM((2 * elements, width), bf16)] * 3
        + [pltpu.VMEM((elements, 2 * elements), bf16)] * 3,
        name="adapt",
    )(*on_chip)


def channel_kernel(
    raw_ref, taps_hbm, table_hbm, out_ref, raw, filtered, taps_ref, table_ref, arrived, small
):
    elem_dev = arrived.shape[0]
    get_taps = pltpu.make_async_copy(taps_hbm, taps_ref, small.at[0])
    get_table = pltpu.make_async_copy(table_hbm, table_ref, small.at[1])
    get_taps.start()
    dests, bin_dev, lanes = out_ref.shape
    rows = lanes // 2
    gate_dev = rows // elem_dev
    per = gate_dev * 8 * TAPS
    copies = [
        pltpu.make_async_copy(
            raw_ref.at[pl.ds(e * per, per)], raw.at[pl.ds(e * per, per)], arrived.at[e]
        )
        for e in range(elem_dev)
    ]
    for copy in copies:
        copy.start()
    get_table.start()
    get_taps.wait()
    pair = lax.broadcasted_iota(jnp.int32, (8, LANES), 0) // 2
    weights = []
    for t in range(TAPS):
        weight = jnp.zeros((8, LANES), jnp.float32)
        for j in range(CHANNELS // LANES):
            piece = taps_ref[t : t + 1, j * LANES : (j + 1) * LANES]
            weight = jnp.where(pair == j, piece, weight)
        weights.append(weight)
    for e, copy in enumerate(copies):
        copy.wait()
        for g in range(gate_dev):
            at = e * per + g * 8 * TAPS
            piece = raw[at : at + 8 * TAPS].astype(jnp.float32)
            total = piece[0:8] * weights[0]
            for t in range(1, TAPS):
                total = total + piece[8 * t : 8 * t + 8] * weights[t]
            to = (g * elem_dev + e) * 8
            filtered[to : to + 8] = total.astype(jnp.bfloat16).astype(jnp.float32)
    get_table.wait()
    sums = []
    for r in range(2):
        rows_r = jnp.concatenate(
            [filtered[pl.ds(2 * j + r, rows, stride=8)] for j in range(CHANNELS // LANES)], axis=1
        ).astype(jnp.bfloat16)
        sums.append(mm(table_ref[...], rows_r, NT, None))
    half = dests * bin_dev
    re = sums[0][:half] + sums[1][half:]
    im = sums[1][:half] - sums[0][half:]
    spectra = jnp.concatenate([re, im], axis=1).astype(jnp.bfloat16)
    for d in range(dests):
        out_ref[d] = spectra[bin_dev * d : bin_dev * (d + 1)]


def channelize(raw_samples, filter_taps, bin_dev, dop_count):
    elem_dev, gate_dev = raw_samples.shape[:2]
    tiles = CHANNELS // LANES
    flat = raw_samples.reshape(elem_dev, gate_dev, 2, TAPS * tiles, LANES)
    flat = jnp.transpose(flat, (0, 1, 3, 2, 4)).reshape(-1, LANES)
    rows = gate_dev * elem_dev
    table = dft_rows(dop_count * bin_dev)
    return pl.pallas_call(
        channel_kernel,
        in_specs=[pl.BlockSpec(memory_space=pl.ANY)] * 3,
        out_specs=pl.BlockSpec(memory_space=pltpu.VMEM),
        out_shape=pltpu.VMEM((dop_count, bin_dev, 2 * rows), jnp.bfloat16),
        scratch_shapes=[
            pltpu.VMEM(flat.shape, jnp.bfloat16),
            pltpu.VMEM((rows * 8, LANES), jnp.float32),
            pltpu.VMEM(filter_taps.shape, jnp.float32),
            pltpu.VMEM(table.shape, jnp.bfloat16),
            pltpu.SemaphoreType.DMA((elem_dev,)),
            pltpu.SemaphoreType.DMA((2,)),
        ],
        name="channelize",
    )(flat, filter_taps, table)


def steering_rows(steer_row, elements):
    element = jnp.arange(elements, dtype=jnp.int32)
    turn = jnp.mod(
        element[None, :] * (2 * steer_row[:, None] - elements), 2 * elements
    ).astype(jnp.float32)
    phases = turn * (math.pi / elements)
    pad = ((0, 8 - steer_row.shape[0]), (0, 0))
    return jnp.pad(jnp.cos(phases), pad), jnp.pad(jnp.sin(phases), pad)


def shards(raw_samples, filter_taps, range_code, train_mask, steer_index):
    elem_dev, gate_dev = raw_samples.shape[:2]
    bin_dev, beams = steer_index.shape
    dop_count, rng_count = lax.axis_size("dop"), lax.axis_size("rng")
    elements = elem_dev * dop_count
    spectra = channelize(raw_samples, filter_taps, bin_dev, dop_count)
    turned = lax.all_to_all(spectra, "dop", split_axis=0, concat_axis=0, tiled=True)
    turned = turned.reshape(dop_count, bin_dev, 2 * gate_dev, elem_dev)
    turned = jnp.transpose(turned, (1, 2, 0, 3)).reshape(bin_dev, 2 * gate_dev, elements)
    mask = jnp.pad(
        train_mask.astype(jnp.bfloat16), ((0, MASK_ROWS - bin_dev), (0, elements - gate_dev))
    )
    turned = turned.reshape(-1, MASK_ROWS, elements)
    chunk = jnp.concatenate([turned, mask[None]], axis=0)
    chunks = lax.all_gather(chunk, "rng", axis=0, tiled=False)
    core = lax.axis_index("rng") % bin_dev
    steer_row = lax.dynamic_index_in_dim(steer_index, core, 0, keepdims=False)
    steer_re, steer_im = steering_rows(steer_row, elements)
    own, other = adapt(range_code, chunks, steer_re, steer_im, bin_dev, beams)
    swapped = lax.ppermute(other, "rng", [(i, i ^ 1) for i in range(rng_count)])
    return own + swapped


def solution(mesh):
    return jax.shard_map(
        shards,
        mesh=mesh,
        in_specs=(P("dop", "rng", None, None), P(), P(), P("dop", "rng"), P("dop", None)),
        out_specs=P(None, "dop", None, "rng"),
        check_vma=False,
    )
```
